32 devices in a mesh: frow: 8 (over z, y), fcol: 4 (over x, core).
Axes of the slice: x: 2, y: 2, z: 4, core: 2. Of those that a mesh axis runs over, the one named last changes fastest.
Arguments:
- image: bfloat16 [2, 4096, 2048], P(None, 'frow', 'fcol'), may hold values from -6 to 6
- window_rows: float32 [4096], P('frow'), may hold values from 0.1 to 1.9
- window_cols: float32 [2048], P('fcol'), may hold values from 0.1 to 1.9
- w_terms: float32 [2], replicated, may hold values from 20 to 200
- facet_row_offset: int32 [8], replicated, may hold values from 0 to 65535
- facet_col_offset: int32 [4], replicated, may hold values from 0 to 65535
- band_offset: int32 [2], replicated, may hold values from 0 to 65535
- sub_row_offset: int32 [2], replicated, may hold values from 0 to 65535
- sub_column: int32 [2], replicated, may hold values from 0 to 1, as said below
Outputs:
- subgrids: float32 [2, 2, 512, 512], P(None, None, 'frow', 'fcol')
The draws below stay inside these ranges and needn't reach their ends.
Inputs may be any that keep to these rules, and one draw needn't show every extreme that they name: `sub_column`: every subgrid column holds exactly 1 subgrids.
All inputs are finite; a program needn't handle non-finite values.
Results may differ from the reference program's by a relative error of at most 0.0052.
Values sent between devices are 32-bit elements; how exact they have to be, the bound alone decides.
A program may use at most 64 MiB of HBM per device.

```python
import math
import jax
import jax.numpy as jnp
from jax import lax

F = 512
SG = 512
IMAGE = 65536
COLS = 2
SUB = 2
NX = 4096
NY = 2048
N_FROW = 8
N_FCOL = 4


def draw_sub_column(key, part):
    order = jax.random.permutation(jax.random.fold_in(key, 17), SUB)
    return (order % COLS).astype(jnp.int32)


def plant(result, stream_key, low, high):
    longest = result.shape.index(max(result.shape))
    spots = []
    for shift in (0, 1):
        where = [jax.random.randint(jax.random.fold_in(stream_key, axis), (), 0, length) for axis, length in enumerate(result.shape)]
        where[longest] = (where[longest] + shift) % result.shape[longest]
        spots.append(tuple(where))
    return result.at[spots[0]].set(low).at[spots[1]].set(high)


def level_of(stream_key, shape, shards, low, high):
    def one(axis_at, blocks):
        draws = jax.random.uniform(jax.random.fold_in(jax.random.fold_in(stream_key, 6), axis_at), (blocks,), jnp.float32, low / len(shards), high / len(shards))
        return jnp.repeat(jnp.exp(draws), shape[axis_at] // blocks).reshape((-1,) + (1,) * (len(shape) - axis_at - 1))

    gain = one(*shards[0])
    for cut in shards[1:]:
        gain = gain * one(*cut)
    return gain


def gaussian(key, shape, width, limit, split=(), kind=jnp.bfloat16):
    level = level_of(key, shape, split, -0.22, 0.18) if split else 1.0
    result = jax.random.normal(key, shape, jnp.float32) * width * level
    return jnp.minimum(jnp.maximum(result, -limit), limit).astype(kind)


def setup_inputs(seed: int = 0) -> dict:
    arg_keys = jax.random.split(jax.random.key(seed), 10)
    return {
        "image": gaussian(arg_keys[0], (2, NX, NY), 1.0, 6.0, ((1, 8), (2, 4))),
        "window_rows": jnp.clip(1.0 + 0.18 * jax.random.normal(arg_keys[1], (NX,), jnp.float32), 0.1, 1.9),
        "window_cols": jnp.clip(1.0 + 0.18 * jax.random.normal(arg_keys[2], (NY,), jnp.float32), 0.1, 1.9),
        "w_terms": jnp.clip(jax.random.uniform(arg_keys[3], (COLS,), jnp.float32, 20.0, 200.0), 20.0, 200.0),
        "facet_row_offset": plant(jax.random.randint(arg_keys[4], (N_FROW,), 0, IMAGE), jax.random.fold_in(arg_keys[4], 1), 0, IMAGE - 1).astype(jnp.int32),
        "facet_col_offset": plant(jax.random.randint(arg_keys[5], (N_FCOL,), 0, IMAGE), jax.random.fold_in(arg_keys[5], 1), 0, IMAGE - 1).astype(jnp.int32),
        "band_offset": jax.random.randint(arg_keys[6], (COLS,), 0, IMAGE).astype(jnp.int32),
        "sub_row_offset": jax.random.randint(arg_keys[7], (SUB,), 0, IMAGE).astype(jnp.int32),
        "sub_column": draw_sub_column(jax.random.fold_in(arg_keys[9], 71), 0),
    }


def phase_index(first, second):
    high = first * (second // 256) % 256 * 256
    return (high + first * (second % 256)) % 65536

def dft_table(coords, freqs):
    angle = phase_index(coords, freqs).astype(jnp.float32) * (2.0 * math.pi / IMAGE)
    return (jnp.cos(angle).astype(jnp.bfloat16), (-jnp.sin(angle)).astype(jnp.bfloat16))

def coord_unit(coords):
    return (coords % IMAGE).astype(jnp.float32) / IMAGE - 0.5

def prepare(real_part, imag_part, wrow, wcol, grow, gcol, w_value):
    lcoord = coord_unit(grow)
    mcoord = coord_unit(gcol)
    angle = w_value * (lcoord[:, None] ** 2 + mcoord[None, :] ** 2)
    scale = wrow[:, None] * wcol[None, :]
    first = real_part.astype(jnp.float32) * scale
    second = imag_part.astype(jnp.float32) * scale
    cosine = jnp.cos(angle)
    sine = jnp.sin(angle)
    return ((first * cosine - second * sine).astype(jnp.bfloat16), (first * sine + second * cosine).astype(jnp.bfloat16))

def matmul(left, right):
    return jnp.dot(left.astype(jnp.float32), right.astype(jnp.float32), precision=lax.Precision.HIGHEST)

def reference(image, window_rows, window_cols, w_terms, facet_row_offset, facet_col_offset, band_offset, sub_row_offset, sub_column):
    local = jnp.arange(F, dtype=jnp.int32)
    freq_base = jnp.arange(SG, dtype=jnp.int32)

    def row_step(total, row_index):
        wrow = lax.dynamic_slice(window_rows, ((row_index * F).astype(jnp.int32),), (F,))
        grow = facet_row_offset[row_index] + local

        def col_step(acc, col_index):
            pixels = lax.dynamic_slice(image, (jnp.int32(0), (row_index * F).astype(jnp.int32), (col_index * F).astype(jnp.int32)), (2, F, F))
            wcol = lax.dynamic_slice(window_cols, ((col_index * F).astype(jnp.int32),), (F,))
            gcol = facet_col_offset[col_index] + local
            pieces = []
            for column in range(COLS):
                prep_re, prep_im = prepare(pixels[0], pixels[1], wrow, wcol, grow, gcol, w_terms[column])
                table_re, table_im = dft_table(gcol[:, None], band_offset[column] + freq_base[None, :])
                out_re = matmul(prep_re, table_re) - matmul(prep_im, table_im)
                out_im = matmul(prep_re, table_im) + matmul(prep_im, table_re)
                pieces.append(jnp.stack([out_re, out_im], axis=1))
            return (acc + jnp.stack(pieces, axis=1), None)
        summed, _ = lax.scan(col_step, jnp.zeros((F, COLS, 2, SG), jnp.float32), jnp.arange(N_FCOL, dtype=jnp.int32))
        banded = (summed / math.sqrt(NY)).astype(jnp.bfloat16)
        results = []
        for sub_index in range(SUB):
            table_re, table_im = dft_table(grow[:, None], sub_row_offset[sub_index] + freq_base[None, :])
            chosen = banded[:, sub_column[sub_index]]
            band_re = chosen[:, 0]
            band_im = chosen[:, 1]
            out_re = matmul(table_re.T, band_re) - matmul(table_im.T, band_im)
            out_im = matmul(table_re.T, band_im) + matmul(table_im.T, band_re)
            results.append(jnp.stack([out_re, out_im], axis=0))
        return (total + jnp.stack(results, axis=0) / math.sqrt(NX), None)
    subgrids, _ = lax.scan(row_step, jnp.zeros((SUB, 2, SG, SG), jnp.float32), jnp.arange(N_FROW, dtype=jnp.int32))
    return subgrids
```

```python
import functools
import math

import jax
import jax.numpy as jnp
from jax import lax
from jax.experimental import pallas as pl
from jax.experimental.pallas import tpu as pltpu
from jax.sharding import PartitionSpec as P

SG = 512
IMAGE = 65536


def phase_index(first, second):
    high = first * (second // 256) % 256 * 256
    return (high + first * (second % 256)) % 65536


def dft_table(coords, freqs):
    angle = phase_index(coords, freqs).astype(jnp.float32) * (2.0 * math.pi / IMAGE)
    return (jnp.cos(angle).astype(jnp.bfloat16), (-jnp.sin(angle)).astype(jnp.bfloat16))


def coord_unit(coords):
    return (coords % IMAGE).astype(jnp.float32) / IMAGE - 0.5


def block_table(table_re, table_im):
    upper = jnp.concatenate([table_re, table_im], axis=1)
    lower = jnp.concatenate([-table_im, table_re], axis=1)
    return jnp.concatenate([upper, lower], axis=0)


def general_local(
    image,
    window_rows,
    window_cols,
    w_terms,
    facet_row_offset,
    facet_col_offset,
    band_offset,
    sub_row_offset,
    sub_column,
):
    facet = image.shape[1]
    column_count = band_offset.shape[0]
    sub_count = sub_row_offset.shape[0]
    frow_index = lax.axis_index("frow")
    fcol_index = lax.axis_index("fcol")
    freq_base = jnp.arange(SG, dtype=jnp.int32)
    gcol = facet_col_offset[fcol_index] + jnp.arange(image.shape[2], dtype=jnp.int32)
    mcoord = coord_unit(gcol)
    row_base = facet_row_offset[frow_index]
    row_ids = row_base + jnp.arange(facet, dtype=jnp.int32)
    radius = coord_unit(row_ids)[:, None] ** 2 + mcoord[None, :] ** 2
    scale = window_rows[:, None] * window_cols[None, :]
    first = image[0].astype(jnp.float32) * scale
    second = image[1].astype(jnp.float32) * scale
    prepared = []
    for column in range(column_count):
        angle = w_terms[column] * radius
        cosine = jnp.cos(angle)
        sine = jnp.sin(angle)
        prep_re = (first * cosine - second * sine).astype(jnp.bfloat16)
        prep_im = (first * sine + second * cosine).astype(jnp.bfloat16)
        prepared.append(jnp.concatenate([prep_re, prep_im], axis=1))
    band_dev = SG // lax.axis_size("fcol")
    freqs = jnp.arange(band_dev * lax.axis_size("fcol"), dtype=jnp.int32)
    outputs = []
    for column in range(column_count):
        table_re, table_im = dft_table(gcol[:, None], band_offset[column] + freqs[None, :])
        whole_table = block_table(table_re, table_im)
        product = lax.dot_general(
            whole_table,
            prepared[column],
            (((0,), (1,)), ((), ())),
            preferred_element_type=jnp.float32,
        )
        outputs.append(
            product.reshape(2, band_dev * lax.axis_size("fcol"), facet).transpose(1, 0, 2)
        )
    summed = lax.psum_scatter(jnp.stack(outputs, axis=1), "fcol", scatter_dimension=0, tiled=True)
    banded = (summed / math.sqrt(facet * lax.axis_size("fcol"))).astype(jnp.bfloat16)
    chosen = jnp.take(banded, sub_column, axis=1)
    right_side = chosen.transpose(1, 2, 3, 0).reshape(sub_count, 2 * facet, band_dev)
    table_re, table_im = dft_table(
        row_ids[None, :, None], sub_row_offset[:, None, None] + freq_base[None, None, :]
    )
    left_real = jnp.concatenate([table_re, -table_im], axis=1)
    left_imag = jnp.concatenate([table_im, table_re], axis=1)
    left_side = jnp.stack([left_real, left_imag], axis=2)
    term = jnp.einsum("kxcu,kxv->kcuv", left_side, right_side, preferred_element_type=jnp.float32)
    term = term * (1.0 / math.sqrt(facet * lax.axis_size("frow")))
    return lax.psum_scatter(term, "frow", scatter_dimension=2, tiled=True)


MESH = pl.DeviceIdType.MESH
TAU = 2.0 * math.pi
ROW_TERMS = 8
COL_TERMS = 16
HALF = ROW_TERMS // 2
BESSEL_STEPS = 8


def remainder(half_facet, half_block, terms):
    z_max = TAU * half_facet * half_block / IMAGE
    return 2.0 * (z_max / 2.0) ** terms / math.factorial(terms)


def iota(shape, axis):
    return lax.broadcasted_iota(jnp.int32, shape, axis)


def turn(index):
    return (index & (IMAGE - 1)).astype(jnp.float32) * (1.0 / IMAGE)


def phasor(turns):
    quadrant = jnp.floor(turns * 4.0 + 0.5)
    t = (turns - quadrant * 0.25) * TAU
    s = t * t
    sine = t * (1.0 + s * (-1 / 6 + s * (1 / 120 + s * (-1 / 5040 + s * (1 / 362880)))))
    cosine = 1.0 + s * (-1 / 2 + s * (1 / 24 + s * (-1 / 720 + s * (1 / 40320 + s * (-1 / 3628800)))))
    q = quadrant.astype(jnp.int32)
    odd = (q & 1) == 1
    real = jnp.where(odd, sine, cosine)
    imag = jnp.where(odd, cosine, sine)
    real = jnp.where(((q + 1) & 2) == 2, -real, real)
    imag = jnp.where((q & 2) == 2, -imag, imag)
    return real, imag


def coord_square(coords):
    unit = (coords & (IMAGE - 1)).astype(jnp.float32) * (1.0 / IMAGE) - 0.5
    return unit * unit


def bessel(order, z, terms):
    half = z * 0.5
    q = half * half
    lead = jnp.where(order == 0, 1.0, 2.0)
    for i in range(1, terms):
        lead = jnp.where(order >= i, lead * half * (1.0 / i), lead)
    tail = jnp.ones_like(z)
    for j in range(BESSEL_STEPS, 0, -1):
        tail = 1.0 - tail * q / (j * (order + j)).astype(jnp.float32)
    return lead * tail


def split(value):
    high = value.astype(jnp.bfloat16)
    return high, (value - high.astype(jnp.float32)).astype(jnp.bfloat16)


def fused_kernel(
    dims,
    image_hbm, wrow_hbm, wcol_hbm, w_hbm, row_off_hbm, col_off_hbm, band_hbm, sub_off_hbm, sub_col_hbm,
    out_ref,
    left, right, rtab, cheb, rphase, cphase, inner, outbox, inbox, vmat, umat,
    wrow_ref, wcol_ref, w_ref, row_off_ref, col_off_ref, band_ref, sub_off_ref, sub_col_ref,
    isem, lsem, osem, ssem, rsem,
):
    n_row, n_col, n_sub, facet, sg, chunks = dims
    r = lax.axis_index("frow")
    c = lax.axis_index("fcol")
    ub, vb = sg // n_row, sg // n_col
    center = facet // 2
    wide = n_col * COL_TERMS
    deep = n_row * ROW_TERMS
    f32, b16 = jnp.float32, jnp.bfloat16

    step = facet // chunks
    images = [
        [
            pltpu.make_async_copy(
                image_hbm.at[i, h * step : (h + 1) * step, :],
                left.at[h * step : (h + 1) * step, i * facet : (i + 1) * facet],
                isem.at[h, i],
            )
            for i in range(2)
        ]
        for h in range(chunks)
    ]
    smalls = [
        pltpu.make_async_copy(src, dst, lsem.at[i])
        for i, (src, dst) in enumerate(
            [
                (sub_col_hbm, sub_col_ref),
                (w_hbm, w_ref),
                (band_hbm, band_ref),
                (sub_off_hbm, sub_off_ref),
                (row_off_hbm, row_off_ref),
                (col_off_hbm, col_off_ref),
                (wrow_hbm, wrow_ref),
                (wcol_hbm, wcol_ref),
            ]
        )
    ]
    for copy in smalls:
        copy.start()
    for pair in images:
        for copy in pair:
            copy.start()

    order = [(dr, dc) for dr in list(range(2, n_row)) + [1, 0] for dc in list(range(1, n_col)) + [0]]
    order = [at for at in order if at != (0, 0)]
    barrier = pltpu.get_barrier_semaphore()
    for dr, dc in order:
        peer = ((r + dr) % n_row, (c + dc) % n_col)
        pl.semaphore_signal(barrier, inc=1, device_id=peer, device_id_type=MESH)

    lane = iota((8, facet), 1)
    local = (lane - center).astype(f32) * (1.0 / center)
    sub = iota((8, facet), 0)
    before, now = jnp.ones_like(local), local
    low = jnp.where(sub == 0, before, now)
    high = low
    for n in range(2, COL_TERMS):
        before, now = now, 2.0 * local * now - before
        if n < 8:
            low = jnp.where(sub == n, now, low)
        else:
            high = jnp.where(sub == n - 8, now, high)
    cheb[0:8, :] = low
    cheb[8:16, :] = high
    for h in range(2):
        part = cheb[HALF * h : HALF * (h + 1), :]
        cheb[16 + 8 * h : 24 + 8 * h, :] = jnp.concatenate([part, part], axis=0)

    for copy in smalls:
        copy.wait()
    columns = [sub_col_ref[k] for k in range(n_sub)]

    def by_sub(index, values):
        out = jnp.full(index.shape, values[0])
        for k in range(1, n_sub):
            out = jnp.where(index == k, values[k], out)
        return out

    waves = [w_ref[columns[k]] * (1.0 / TAU) for k in range(n_sub)]

    def phases(table, coords, n_block, block, firsts, shift, gain):
        row = iota((n_sub * n_block, facet), 0)
        which = row // n_block
        start = by_sub(which, firsts) + ((row + shift) % n_block) * block + block // 2
        turns = by_sub(which, waves) * coord_square(coords) - turn(coords * start)
        re, im = phasor(turns)
        table[0] = re * gain
        table[1] = im * gain

    gcol = col_off_ref[c] + iota((1, facet), 1)
    grow = row_off_ref[r] + iota((1, facet), 1)
    scale = 1.0 / math.sqrt(facet * n_col) / math.sqrt(facet * n_row)
    phases(cphase, gcol, n_col, vb, [band_ref[columns[k]] for k in range(n_sub)], c, wcol_ref[...])
    basis = cheb[0:COL_TERMS, :]
    for k in range(n_sub):
        for p in range(n_col):
            at = k * n_col + p
            re = (cphase[0, at : at + 1, :] * basis).astype(b16)
            im = (cphase[1, at : at + 1, :] * basis).astype(b16)
            top = 2 * wide * k + COL_TERMS * p
            right[top : top + COL_TERMS, :facet] = re
            right[top : top + COL_TERMS, facet:] = -im
            right[top + wide : top + wide + COL_TERMS, :facet] = im
            right[top + wide : top + wide + COL_TERMS, facet:] = re

    phases(rphase, grow, n_row, ub, [sub_off_ref[k] for k in range(n_sub)], 0, wrow_ref[...] * scale)
    first_half = sub < HALF
    for k in range(n_sub):
        for i in range(2):
            for q in range(0, n_row, 4):
                pairs = []
                for b in (q, q + 2):
                    at = k * n_row + b
                    pairs.append(
                        jnp.where(first_half, rphase[i, at : at + 1, :], rphase[i, at + 1 : at + 2, :])
                    )
                for h in range(2):
                    terms = cheb[16 + 8 * h : 24 + 8 * h, :]
                    value = jnp.concatenate([pair * terms for pair in pairs], axis=0).astype(b16)
                    top = i * deep + h * HALF * n_row + HALF * q
                    rtab[k, top : top + 16, :] = value

    for h in range(chunks):
        for copy in images[h]:
            copy.wait()
        rows = slice(h * step, (h + 1) * step)
        inner[rows, :] = lax.dot_general(
            left[rows, :], right[...], (((1,), (1,)), ((), ())), preferred_element_type=f32
        ).astype(b16)

    slot = iota((HALF * n_row, 2 * wide), 1) // COL_TERMS
    half_sign = jnp.where(iota((deep, 2 * wide), 1) < wide, -1.0, 1.0)
    turned = []
    for k in range(n_sub):
        product = jnp.dot(
            rtab[k], inner[:, 2 * wide * k : 2 * wide * (k + 1)], preferred_element_type=f32
        )
        moments = product[:deep] + half_sign * pltpu.roll(product[deep:], wide, 1)
        for h in range(2):
            g = 2 * k + h
            value = moments[HALF * n_row * h : HALF * n_row * (h + 1)]
            turned.append(value if g == 0 else pltpu.roll(value, COL_TERMS * g, 1))
    for d in range(n_col):
        box = turned[0]
        for g in range(1, n_col):
            box = jnp.where(slot % n_col == (d + g) % n_col, turned[g], box)
        outbox[d] = box

    mine = pl.ds(HALF * r, HALF)
    own = pltpu.make_async_copy(outbox.at[0, mine, :], inbox.at[0, mine, :], osem)
    own.start()
    pl.semaphore_wait(barrier, n_row * n_col - 1)
    copies = []
    for dr, dc in order:
        to = (r + dr) % n_row
        copy = pltpu.make_async_remote_copy(
            src_ref=outbox.at[dc, pl.ds(HALF * to, HALF), :],
            dst_ref=inbox.at[dc, mine, :],
            send_sem=ssem.at[dr, dc],
            recv_sem=rsem.at[dr, dc],
            device_id=(to, (c + dc) % n_col),
            device_id_type=MESH,
        )
        copy.start()
        copies.append(copy)

    row = iota((wide, vb), 0)
    off = iota((wide, vb), 1) - vb // 2
    which, term = row // COL_TERMS, row % COL_TERMS
    start = jnp.full((wide, vb), center)
    for p in range(n_col):
        start = jnp.where(which == p, col_off_ref[(c + n_col - p) % n_col] + center, start)
    re, im = phasor(-turn(start * off) - 0.25 * (term % 4).astype(f32))
    size = bessel(term, off.astype(f32) * (TAU * center / IMAGE), COL_TERMS)
    re, im = re * size, im * size
    table = jnp.concatenate(
        [jnp.concatenate([re, im], axis=1), jnp.concatenate([-im, re], axis=1)], axis=0
    )
    high_part, low_part = split(table)
    vmat[0 : 2 * wide, :] = high_part
    vmat[2 * wide : 4 * wide, :] = high_part
    vmat[4 * wide : 6 * wide, :] = low_part

    lanes = iota((ub, deep), 1)
    off = iota((ub, deep), 0) - ub // 2
    which = lanes // HALF % n_row
    term = lanes // (HALF * n_row) * HALF + lanes % HALF
    start = jnp.full((ub, deep), center)
    for b in range(n_row):
        start = jnp.where(which == b, row_off_ref[b] + center, start)
    re, im = phasor(-turn(start * off) - 0.25 * (term % 4).astype(f32))
    size = bessel(term, off.astype(f32) * (TAU * center / IMAGE), ROW_TERMS)
    for i, part in enumerate((re * size, im * size)):
        high_part, low_part = split(part)
        rows = slice(i * ub, (i + 1) * ub)
        umat[rows, 0:deep] = high_part
        umat[rows, deep : 2 * deep] = low_part
        umat[rows, 2 * deep : 3 * deep] = high_part

    own.wait()
    for copy in copies:
        copy.wait_recv()

    boxes = [inbox[d] for d in range(n_col)]
    for k in range(n_sub):
        halves = []
        for h in range(2):
            g = 2 * k + h
            value = boxes[0]
            for d in range(1, n_col):
                value = jnp.where(slot % n_col == (d + g) % n_col, boxes[d], value)
            halves.append(value if g == 0 else pltpu.roll(value, 2 * wide - COL_TERMS * g, 1))
        high_part, low_part = split(jnp.concatenate(halves, axis=0))
        x = jnp.dot(
            jnp.concatenate([high_part, low_part, high_part], axis=1),
            vmat[...],
            preferred_element_type=f32,
        )
        high_part, low_part = split(x)
        y = jnp.dot(
            umat[...],
            jnp.concatenate([high_part, high_part, low_part], axis=0),
            preferred_element_type=f32,
        )
        out_ref[k, 0] = y[:ub, :vb] - y[ub:, vb:]
        out_ref[k, 1] = y[:ub, vb:] + y[ub:, :vb]
    for copy in copies:
        copy.wait_send()


def fused_local(n_row, n_col, image, *rest):
    facet = image.shape[1]
    n_sub = rest[6].shape[0]
    chunks = 2
    wide, deep = n_col * COL_TERMS, n_row * ROW_TERMS
    ub, vb = SG // n_row, SG // n_col
    f32, b16, i32 = jnp.float32, jnp.bfloat16, jnp.int32
    vmem, smem, dma = pltpu.VMEM, pltpu.SMEM, pltpu.SemaphoreType.DMA
    rest = [rest[0].reshape(1, -1), rest[1].reshape(1, -1), *rest[2:]]
    return pl.pallas_call(
        functools.partial(fused_kernel, (n_row, n_col, n_sub, facet, SG, chunks)),
        out_shape=jax.ShapeDtypeStruct((n_sub, 2, ub, vb), f32),
        in_specs=[pl.BlockSpec(memory_space=pl.ANY)] * 9,
        out_specs=pl.BlockSpec(memory_space=vmem),
        scratch_shapes=[
            vmem((facet, 2 * facet), b16),
            vmem((2 * n_sub * wide, 2 * facet), b16),
            vmem((n_sub, 2 * deep, facet), b16),
            vmem((32, facet), f32),
            vmem((2, n_sub * n_row, facet), f32),
            vmem((2, n_sub * n_col, facet), f32),
            vmem((facet, 2 * n_sub * wide), b16),
            vmem((n_col, HALF * n_row, 2 * wide), f32),
            vmem((n_col, HALF * n_row, 2 * wide), f32),
            vmem((6 * wide, 2 * vb), b16),
            vmem((2 * ub, 3 * deep), b16),
            *[vmem(a.shape, a.dtype) for a in rest[:2]],
            *[smem(a.shape, a.dtype) for a in rest[2:]],
            dma((chunks, 2)),
            dma((8,)),
            dma,
            dma((n_row, n_col)),
            dma((n_row, n_col)),
        ],
        compiler_params=pltpu.CompilerParams(
            collective_id=0, has_side_effects=True, vmem_limit_bytes=56 << 20
        ),
    )(image, *rest)


def solution(mesh):
    n_row, n_col = mesh.shape["frow"], mesh.shape["fcol"]
    ub, vb = SG // n_row, SG // n_col

    def local(image, *rest):
        facet, n_sub = image.shape[1], rest[-1].shape[0]
        tiled = (
            SG == ub * n_row == vb * n_col
            and n_row % 4 == 0
            and n_col == 2 * n_sub
            and n_col * COL_TERMS == 64
            and ub % 8 == 0
            and vb % 128 == 0
            and image.shape[2] == facet
            and facet % 256 == 0
            and remainder(facet // 2, ub // 2, ROW_TERMS) < 2.0**-24
            and remainder(facet // 2, vb // 2, COL_TERMS) < 2.0**-24
        )
        return (functools.partial(fused_local, n_row, n_col) if tiled else general_local)(image, *rest)

    placed = (P(None, "frow", "fcol"), P("frow"), P("fcol"), P(), P(), P(), P(), P(), P())
    return jax.shard_map(
        local, mesh=mesh, in_specs=placed, out_specs=P(None, None, "frow", "fcol"), check_vma=False
    )
```

```python
import functools
import math

import jax
import jax.numpy as jnp
from jax import lax
from jax.experimental import pallas as pl
from jax.experimental.pallas import tpu as pltpu
from jax.sharding import PartitionSpec as P

SG = 512
IMAGE = 65536


def phase_index(first, second):
    high = first * (second // 256) % 256 * 256
    return (high + first * (second % 256)) % 65536


def dft_table(coords, freqs):
    angle = phase_index(coords, freqs).astype(jnp.float32) * (2.0 * math.pi / IMAGE)
    return (jnp.cos(angle).astype(jnp.bfloat16), (-jnp.sin(angle)).astype(jnp.bfloat16))


def coord_unit(coords):
    return (coords % IMAGE).astype(jnp.float32) / IMAGE - 0.5


def block_table(table_re, table_im):
    upper = jnp.concatenate([table_re, table_im], axis=1)
    lower = jnp.concatenate([-table_im, table_re], axis=1)
    return jnp.concatenate([upper, lower], axis=0)


def general_local(
    image,
    window_rows,
    window_cols,
    w_terms,
    facet_row_offset,
    facet_col_offset,
    band_offset,
    sub_row_offset,
    sub_column,
):
    facet = image.shape[1]
    column_count = band_offset.shape[0]
    sub_count = sub_row_offset.shape[0]
    frow_index = lax.axis_index("frow")
    fcol_index = lax.axis_index("fcol")
    freq_base = jnp.arange(SG, dtype=jnp.int32)
    gcol = facet_col_offset[fcol_index] + jnp.arange(image.shape[2], dtype=jnp.int32)
    mcoord = coord_unit(gcol)
    row_base = facet_row_offset[frow_index]
    row_ids = row_base + jnp.arange(facet, dtype=jnp.int32)
    radius = coord_unit(row_ids)[:, None] ** 2 + mcoord[None, :] ** 2
    scale = window_rows[:, None] * window_cols[None, :]
    first = image[0].astype(jnp.float32) * scale
    second = image[1].astype(jnp.float32) * scale
    prepared = []
    for column in range(column_count):
        angle = w_terms[column] * radius
        cosine = jnp.cos(angle)
        sine = jnp.sin(angle)
        prep_re = (first * cosine - second * sine).astype(jnp.bfloat16)
        prep_im = (first * sine + second * cosine).astype(jnp.bfloat16)
        prepared.append(jnp.concatenate([prep_re, prep_im], axis=1))
    band_dev = SG // lax.axis_size("fcol")
    freqs = jnp.arange(band_dev * lax.axis_size("fcol"), dtype=jnp.int32)
    outputs = []
    for column in range(column_count):
        table_re, table_im = dft_table(gcol[:, None], band_offset[column] + freqs[None, :])
        whole_table = block_table(table_re, table_im)
        product = lax.dot_general(
            whole_table,
            prepared[column],
            (((0,), (1,)), ((), ())),
            preferred_element_type=jnp.float32,
        )
        outputs.append(
            product.reshape(2, band_dev * lax.axis_size("fcol"), facet).transpose(1, 0, 2)
        )
    summed = lax.psum_scatter(jnp.stack(outputs, axis=1), "fcol", scatter_dimension=0, tiled=True)
    banded = (summed / math.sqrt(facet * lax.axis_size("fcol"))).astype(jnp.bfloat16)
    chosen = jnp.take(banded, sub_column, axis=1)
    right_side = chosen.transpose(1, 2, 3, 0).reshape(sub_count, 2 * facet, band_dev)
    table_re, table_im = dft_table(
        row_ids[None, :, None], sub_row_offset[:, None, None] + freq_base[None, None, :]
    )
    left_real = jnp.concatenate([table_re, -table_im], axis=1)
    left_imag = jnp.concatenate([table_im, table_re], axis=1)
    left_side = jnp.stack([left_real, left_imag], axis=2)
    term = jnp.einsum("kxcu,kxv->kcuv", left_side, right_side, preferred_element_type=jnp.float32)
    term = term * (1.0 / math.sqrt(facet * lax.axis_size("frow")))
    return lax.psum_scatter(term, "frow", scatter_dimension=2, tiled=True)


MESH = pl.DeviceIdType.MESH
TAU = 2.0 * math.pi
ROW_TERMS = 8
COL_TERMS = 16
HALF = ROW_TERMS // 2
BESSEL_STEPS = 8


def remainder(half_facet, half_block, terms):
    z_max = TAU * half_facet * half_block / IMAGE
    return 2.0 * (z_max / 2.0) ** terms / math.factorial(terms)


def iota(shape, axis):
    return lax.broadcasted_iota(jnp.int32, shape, axis)


def turn(index):
    return (index & (IMAGE - 1)).astype(jnp.float32) * (1.0 / IMAGE)


def phasor(turns):
    quadrant = jnp.floor(turns * 4.0 + 0.5)
    t = (turns - quadrant * 0.25) * TAU
    s = t * t
    sine = t * (1.0 + s * (-1 / 6 + s * (1 / 120 + s * (-1 / 5040 + s * (1 / 362880)))))
    cosine = 1.0 + s * (-1 / 2 + s * (1 / 24 + s * (-1 / 720 + s * (1 / 40320 + s * (-1 / 3628800)))))
    q = quadrant.astype(jnp.int32)
    odd = (q & 1) == 1
    real = jnp.where(odd, sine, cosine)
    imag = jnp.where(odd, cosine, sine)
    real = jnp.where(((q + 1) & 2) == 2, -real, real)
    imag = jnp.where((q & 2) == 2, -imag, imag)
    return real, imag


def coord_square(coords):
    unit = (coords & (IMAGE - 1)).astype(jnp.float32) * (1.0 / IMAGE) - 0.5
    return unit * unit


def bessel(order, z, terms):
    half = z * 0.5
    q = half * half
    lead = jnp.where(order == 0, 1.0, 2.0)
    for i in range(1, terms):
        lead = jnp.where(order >= i, lead * half * (1.0 / i), lead)
    tail = jnp.ones_like(z)
    for j in range(BESSEL_STEPS, 0, -1):
        tail = 1.0 - tail * q / (j * (order + j)).astype(jnp.float32)
    return lead * tail


def split(value):
    high = value.astype(jnp.bfloat16)
    return high, (value - high.astype(jnp.float32)).astype(jnp.bfloat16)


def fused_kernel(
    dims,
    image_hbm, wrow_hbm, wcol_hbm, w_hbm, row_off_hbm, col_off_hbm, band_hbm, sub_off_hbm, sub_col_hbm,
    out_ref,
    left, right, rtab, cheb, rphase, cphase, inner, outbox, inbox, vmat, umat,
    wrow_ref, wcol_ref, w_ref, row_off_ref, col_off_ref, band_ref, sub_off_ref, sub_col_ref,
    isem, lsem, osem, ssem, rsem,
):
    n_row, n_col, n_sub, facet, sg, chunks = dims
    r = lax.axis_index("frow")
    c = lax.axis_index("fcol")
    ub, vb = sg // n_row, sg // n_col
    center = facet // 2
    wide = n_col * COL_TERMS
    deep = n_row * ROW_TERMS
    f32, b16 = jnp.float32, jnp.bfloat16

    step = facet // chunks
    images = [
        [
            pltpu.make_async_copy(
                image_hbm.at[i, h * step : (h + 1) * step, :],
                left.at[h * step : (h + 1) * step, i * facet : (i + 1) * facet],
                isem.at[h, i],
            )
            for i in range(2)
        ]
        for h in range(chunks)
    ]
    smalls = [
        pltpu.make_async_copy(src, dst, lsem.at[i])
        for i, (src, dst) in enumerate(
            [
                (sub_col_hbm, sub_col_ref),
                (w_hbm, w_ref),
                (band_hbm, band_ref),
                (sub_off_hbm, sub_off_ref),
                (row_off_hbm, row_off_ref),
                (col_off_hbm, col_off_ref),
                (wrow_hbm, wrow_ref),
                (wcol_hbm, wcol_ref),
            ]
        )
    ]
    for copy in smalls:
        copy.start()
    for pair in images:
        for copy in pair:
            copy.start()

    order = [(dr, dc) for dr in list(range(2, n_row)) + [1, 0] for dc in list(range(1, n_col)) + [0]]
    order = [at for at in order if at != (0, 0)]
    barrier = pltpu.get_barrier_semaphore()
    for dr, dc in order:
        peer = ((r + dr) % n_row, (c + dc) % n_col)
        pl.semaphore_signal(barrier, inc=1, device_id=peer, device_id_type=MESH)

    lane = iota((8, facet), 1)
    local = (lane - center).astype(f32) * (1.0 / center)
    sub = iota((8, facet), 0)
    before, now = jnp.ones_like(local), local
    low = jnp.where(sub == 0, before, now)
    high = low
    for n in range(2, COL_TERMS):
        before, now = now, 2.0 * local * now - before
        if n < 8:
            low = jnp.where(sub == n, now, low)
        else:
            high = jnp.where(sub == n - 8, now, high)
    cheb[0:8, :] = low
    cheb[8:16, :] = high
    for h in range(2):
        part = cheb[HALF * h : HALF * (h + 1), :]
        cheb[16 + 8 * h : 24 + 8 * h, :] = jnp.concatenate([part, part], axis=0)

    for copy in smalls:
        copy.wait()
    columns = [sub_col_ref[k] for k in range(n_sub)]

    def by_sub(index, values):
        out = jnp.full(index.shape, values[0])
        for k in range(1, n_sub):
            out = jnp.where(index == k, values[k], out)
        return out

    waves = [w_ref[columns[k]] * (1.0 / TAU) for k in range(n_sub)]

    def phases(table, coords, n_block, block, firsts, shift, gain):
        row = iota((n_sub * n_block, facet), 0)
        which = row // n_block
        start = by_sub(which, firsts) + ((row + shift) % n_block) * block + block // 2
        turns = by_sub(which, waves) * coord_square(coords) - turn(coords * start)
        re, im = phasor(turns)
        table[0] = re * gain
        table[1] = im * gain

    gcol = col_off_ref[c] + iota((1, facet), 1)
    grow = row_off_ref[r] + iota((1, facet), 1)
    scale = 1.0 / math.sqrt(facet * n_col) / math.sqrt(facet * n_row)
    phases(cphase, gcol, n_col, vb, [band_ref[columns[k]] for k in range(n_sub)], c, wcol_ref[...])
    basis = cheb[0:COL_TERMS, :]
    for k in range(n_sub):
        for p in range(n_col):
            at = k * n_col + p
            re = (cphase[0, at : at + 1, :] * basis).astype(b16)
            im = (cphase[1, at : at + 1, :] * basis).astype(b16)
            top = 2 * wide * k + COL_TERMS * p
            right[top : top + COL_TERMS, :facet] = re
            right[top : top + COL_TERMS, facet:] = -im
            right[top + wide : top + wide + COL_TERMS, :facet] = im
            right[top + wide : top + wide + COL_TERMS, facet:] = re

    phases(rphase, grow, n_row, ub, [sub_off_ref[k] for k in range(n_sub)], 0, wrow_ref[...] * scale)
    first_half = sub < HALF
    for k in range(n_sub):
        for i in range(2):
            for q in range(0, n_row, 4):
                pairs = []
                for b in (q, q + 2):
                    at = k * n_row + b
                    pairs.append(
                        jnp.where(first_half, rphase[i, at : at + 1, :], rphase[i, at + 1 : at + 2, :])
                    )
                for h in range(2):
                    terms = cheb[16 + 8 * h : 24 + 8 * h, :]
                    value = jnp.concatenate([pair * terms for pair in pairs], axis=0).astype(b16)
                    top = i * deep + h * HALF * n_row + HALF * q
                    rtab[k, top : top + 16, :] = value

    for h in range(chunks):
        for copy in images[h]:
            copy.wait()
        rows = slice(h * step, (h + 1) * step)
        inner[rows, :] = lax.dot_general(
            left[rows, :], right[...], (((1,), (1,)), ((), ())), preferred_element_type=f32
        ).astype(b16)

    slot = iota((HALF * n_row, 2 * wide), 1) // COL_TERMS
    half_sign = jnp.where(iota((deep, 2 * wide), 1) < wide, -1.0, 1.0)
    turned = []
    for k in range(n_sub):
        product = jnp.dot(
            rtab[k], inner[:, 2 * wide * k : 2 * wide * (k + 1)], preferred_element_type=f32
        )
        moments = product[:deep] + half_sign * pltpu.roll(product[deep:], wide, 1)
        for h in range(2):
            g = 2 * k + h
            value = moments[HALF * n_row * h : HALF * n_row * (h + 1)]
            turned.append(value if g == 0 else pltpu.roll(value, COL_TERMS * g, 1))
    for d in range(n_col):
        box = turned[0]
        for g in range(1, n_col):
            box = jnp.where(slot % n_col == (d + g) % n_col, turned[g], box)
        outbox[d] = box

    mine = pl.ds(HALF * r, HALF)
    own = pltpu.make_async_copy(outbox.at[0, mine, :], inbox.at[0, mine, :], osem)
    own.start()
    pl.semaphore_wait(barrier, n_row * n_col - 1)
    copies = []
    for dr, dc in order:
        to = (r + dr) % n_row
        copy = pltpu.make_async_remote_copy(
            src_ref=outbox.at[dc, pl.ds(HALF * to, HALF), :],
            dst_ref=inbox.at[dc, mine, :],
            send_sem=ssem.at[dr, dc],
            recv_sem=rsem.at[dr, dc],
            device_id=(to, (c + dc) % n_col),
            device_id_type=MESH,
        )
        copy.start()
        copies.append(copy)

    row = iota((wide, vb), 0)
    off = iota((wide, vb), 1) - vb // 2
    which, term = row // COL_TERMS, row % COL_TERMS
    start = jnp.full((wide, vb), center)
    for p in range(n_col):
        start = jnp.where(which == p, col_off_ref[(c + n_col - p) % n_col] + center, start)
    re, im = phasor(-turn(start * off) - 0.25 * (term % 4).astype(f32))
    size = bessel(term, off.astype(f32) * (TAU * center / IMAGE), COL_TERMS)
    re, im = re * size, im * size
    table = jnp.concatenate(
        [jnp.concatenate([re, im], axis=1), jnp.concatenate([-im, re], axis=1)], axis=0
    )
    high_part, low_part = split(table)
    vmat[0 : 2 * wide, :] = high_part
    vmat[2 * wide : 4 * wide, :] = high_part
    vmat[4 * wide : 6 * wide, :] = low_part

    lanes = iota((ub, deep), 1)
    off = iota((ub, deep), 0) - ub // 2
    which = lanes // HALF % n_row
    term = lanes // (HALF * n_row) * HALF + lanes % HALF
    start = jnp.full((ub, deep), center)
    for b in range(n_row):
        start = jnp.where(which == b, row_off_ref[b] + center, start)
    re, im = phasor(-turn(start * off) - 0.25 * (term % 4).astype(f32))
    size = bessel(term, off.astype(f32) * (TAU * center / IMAGE), ROW_TERMS)
    for i, part in enumerate((re * size, im * size)):
        high_part, low_part = split(part)
        rows = slice(i * ub, (i + 1) * ub)
        umat[rows, 0:deep] = high_part
        umat[rows, deep : 2 * deep] = low_part
        umat[rows, 2 * deep : 3 * deep] = high_part

    own.wait()
    for copy in copies:
        copy.wait_recv()

    boxes = [inbox[d] for d in range(n_col)]
    for k in range(n_sub):
        halves = []
        for h in range(2):
            g = 2 * k + h
            value = boxes[0]
            for d in range(1, n_col):
                value = jnp.where(slot % n_col == (d + g) % n_col, boxes[d], value)
            halves.append(value if g == 0 else pltpu.roll(value, 2 * wide - COL_TERMS * g, 1))
        high_part, low_part = split(jnp.concatenate(halves, axis=0))
        x = jnp.dot(
            jnp.concatenate([high_part, low_part, high_part], axis=1),
            vmat[...],
            preferred_element_type=f32,
        )
        high_part, low_part = split(x)
        y = jnp.dot(
            umat[...],
            jnp.concatenate([high_part, high_part, low_part], axis=0),
            preferred_element_type=f32,
        )
        out_ref[k, 0] = y[:ub, :vb] - y[ub:, vb:]
        out_ref[k, 1] = y[:ub, vb:] + y[ub:, :vb]
    for copy in copies:
        copy.wait_send()


def store_kernel(held, out_hbm, sem):
    copy = pltpu.make_async_copy(held, out_hbm, sem)
    copy.start()
    copy.wait()


def fused_local(n_row, n_col, image, *rest):
    facet = image.shape[1]
    n_sub = rest[6].shape[0]
    chunks = 2
    wide, deep = n_col * COL_TERMS, n_row * ROW_TERMS
    ub, vb = SG // n_row, SG // n_col
    f32, b16, i32 = jnp.float32, jnp.bfloat16, jnp.int32
    vmem, smem, dma = pltpu.VMEM, pltpu.SMEM, pltpu.SemaphoreType.DMA
    rest = [rest[0].reshape(1, -1), rest[1].reshape(1, -1), *rest[2:]]
    held = pl.pallas_call(
        functools.partial(fused_kernel, (n_row, n_col, n_sub, facet, SG, chunks)),
        out_shape=vmem((n_sub, 2, ub, vb), f32),
        in_specs=[pl.BlockSpec(memory_space=pl.ANY)] * 9,
        out_specs=pl.BlockSpec(memory_space=vmem),
        scratch_shapes=[
            vmem((facet, 2 * facet), b16),
            vmem((2 * n_sub * wide, 2 * facet), b16),
            vmem((n_sub, 2 * deep, facet), b16),
            vmem((32, facet), f32),
            vmem((2, n_sub * n_row, facet), f32),
            vmem((2, n_sub * n_col, facet), f32),
            vmem((facet, 2 * n_sub * wide), b16),
            vmem((n_col, HALF * n_row, 2 * wide), f32),
            vmem((n_col, HALF * n_row, 2 * wide), f32),
            vmem((6 * wide, 2 * vb), b16),
            vmem((2 * ub, 3 * deep), b16),
            *[vmem(a.shape, a.dtype) for a in rest[:2]],
            *[smem(a.shape, a.dtype) for a in rest[2:]],
            dma((chunks, 2)),
            dma((8,)),
            dma,
            dma((n_row, n_col)),
            dma((n_row, n_col)),
        ],
        compiler_params=pltpu.CompilerParams(
            collective_id=0, has_side_effects=True, vmem_limit_bytes=56 << 20
        ),
    )(image, *rest)
    return held


def solution(mesh):
    n_row, n_col = mesh.shape["frow"], mesh.shape["fcol"]
    ub, vb = SG // n_row, SG // n_col

    def local(image, *rest):
        facet, n_sub = image.shape[1], rest[-1].shape[0]
        tiled = (
            SG == ub * n_row == vb * n_col
            and n_row % 4 == 0
            and n_col == 2 * n_sub
            and n_col * COL_TERMS == 64
            and ub % 8 == 0
            and vb % 128 == 0
            and image.shape[2] == facet
            and facet % 256 == 0
            and remainder(facet // 2, ub // 2, ROW_TERMS) < 2.0**-24
            and remainder(facet // 2, vb // 2, COL_TERMS) < 2.0**-24
        )
        return (functools.partial(fused_local, n_row, n_col) if tiled else general_local)(image, *rest)

    placed = (P(None, "frow", "fcol"), P("frow"), P("fcol"), P(), P(), P(), P(), P(), P())
    return jax.shard_map(
        local, mesh=mesh, in_specs=placed, out_specs=P(None, None, "frow", "fcol"), check_vma=False
    )
```

```python
import functools
import math

import jax
import jax.numpy as jnp
from jax import lax
from jax.experimental import pallas as pl
from jax.experimental.pallas import tpu as pltpu
from jax.sharding import PartitionSpec as P

SG = 512
IMAGE = 65536


def phase_index(first, second):
    high = first * (second // 256) % 256 * 256
    return (high + first * (second % 256)) % 65536


def dft_table(coords, freqs):
    angle = phase_index(coords, freqs).astype(jnp.float32) * (2.0 * math.pi / IMAGE)
    return (jnp.cos(angle).astype(jnp.bfloat16), (-jnp.sin(angle)).astype(jnp.bfloat16))


def coord_unit(coords):
    return (coords % IMAGE).astype(jnp.float32) / IMAGE - 0.5


def block_table(table_re, table_im):
    upper = jnp.concatenate([table_re, table_im], axis=1)
    lower = jnp.concatenate([-table_im, table_re], axis=1)
    return jnp.concatenate([upper, lower], axis=0)


def general_local(
    image,
    window_rows,
    window_cols,
    w_terms,
    facet_row_offset,
    facet_col_offset,
    band_offset,
    sub_row_offset,
    sub_column,
):
    facet = image.shape[1]
    column_count = band_offset.shape[0]
    sub_count = sub_row_offset.shape[0]
    frow_index = lax.axis_index("frow")
    fcol_index = lax.axis_index("fcol")
    freq_base = jnp.arange(SG, dtype=jnp.int32)
    gcol = facet_col_offset[fcol_index] + jnp.arange(image.shape[2], dtype=jnp.int32)
    mcoord = coord_unit(gcol)
    row_base = facet_row_offset[frow_index]
    row_ids = row_base + jnp.arange(facet, dtype=jnp.int32)
    radius = coord_unit(row_ids)[:, None] ** 2 + mcoord[None, :] ** 2
    scale = window_rows[:, None] * window_cols[None, :]
    first = image[0].astype(jnp.float32) * scale
    second = image[1].astype(jnp.float32) * scale
    prepared = []
    for column in range(column_count):
        angle = w_terms[column] * radius
        cosine = jnp.cos(angle)
        sine = jnp.sin(angle)
        prep_re = (first * cosine - second * sine).astype(jnp.bfloat16)
        prep_im = (first * sine + second * cosine).astype(jnp.bfloat16)
        prepared.append(jnp.concatenate([prep_re, prep_im], axis=1))
    band_dev = SG // lax.axis_size("fcol")
    freqs = jnp.arange(band_dev * lax.axis_size("fcol"), dtype=jnp.int32)
    outputs = []
    for column in range(column_count):
        table_re, table_im = dft_table(gcol[:, None], band_offset[column] + freqs[None, :])
        whole_table = block_table(table_re, table_im)
        product = lax.dot_general(
            whole_table,
            prepared[column],
            (((0,), (1,)), ((), ())),
            preferred_element_type=jnp.float32,
        )
        outputs.append(
            product.reshape(2, band_dev * lax.axis_size("fcol"), facet).transpose(1, 0, 2)
        )
    summed = lax.psum_scatter(jnp.stack(outputs, axis=1), "fcol", scatter_dimension=0, tiled=True)
    banded = (summed / math.sqrt(facet * lax.axis_size("fcol"))).astype(jnp.bfloat16)
    chosen = jnp.take(banded, sub_column, axis=1)
    right_side = chosen.transpose(1, 2, 3, 0).reshape(sub_count, 2 * facet, band_dev)
    table_re, table_im = dft_table(
        row_ids[None, :, None], sub_row_offset[:, None, None] + freq_base[None, None, :]
    )
    left_real = jnp.concatenate([table_re, -table_im], axis=1)
    left_imag = jnp.concatenate([table_im, table_re], axis=1)
    left_side = jnp.stack([left_real, left_imag], axis=2)
    term = jnp.einsum("kxcu,kxv->kcuv", left_side, right_side, preferred_element_type=jnp.float32)
    term = term * (1.0 / math.sqrt(facet * lax.axis_size("frow")))
    return lax.psum_scatter(term, "frow", scatter_dimension=2, tiled=True)


MESH = pl.DeviceIdType.MESH
TAU = 2.0 * math.pi
ROW_TERMS = 8
COL_TERMS = 16
HALF = ROW_TERMS // 2
BESSEL_STEPS = 8


def remainder(half_facet, half_block, terms):
    z_max = TAU * half_facet * half_block / IMAGE
    return 2.0 * (z_max / 2.0) ** terms / math.factorial(terms)


def iota(shape, axis):
    return lax.broadcasted_iota(jnp.int32, shape, axis)


def turn(index):
    return (index & (IMAGE - 1)).astype(jnp.float32) * (1.0 / IMAGE)


def phasor(turns):
    quadrant = jnp.floor(turns * 4.0 + 0.5)
    t = (turns - quadrant * 0.25) * TAU
    s = t * t
    sine = t * (1.0 + s * (-1 / 6 + s * (1 / 120 + s * (-1 / 5040 + s * (1 / 362880)))))
    cosine = 1.0 + s * (-1 / 2 + s * (1 / 24 + s * (-1 / 720 + s * (1 / 40320 + s * (-1 / 3628800)))))
    q = quadrant.astype(jnp.int32)
    odd = (q & 1) == 1
    real = jnp.where(odd, sine, cosine)
    imag = jnp.where(odd, cosine, sine)
    real = jnp.where(((q + 1) & 2) == 2, -real, real)
    imag = jnp.where((q & 2) == 2, -imag, imag)
    return real, imag


def coord_square(coords):
    unit = (coords & (IMAGE - 1)).astype(jnp.float32) * (1.0 / IMAGE) - 0.5
    return unit * unit


def bessel(order, z, terms):
    half = z * 0.5
    q = half * half
    lead = jnp.where(order == 0, 1.0, 2.0)
    for i in range(1, terms):
        lead = jnp.where(order >= i, lead * half * (1.0 / i), lead)
    tail = jnp.ones_like(z)
    for j in range(BESSEL_STEPS, 0, -1):
        tail = 1.0 - tail * q / (j * (order + j)).astype(jnp.float32)
    return lead * tail


def split(value):
    high = value.astype(jnp.bfloat16)
    return high, (value - high.astype(jnp.float32)).astype(jnp.bfloat16)


def fused_kernel(
    dims,
    image_hbm, wrow_hbm, wcol_hbm, w_hbm, row_off_hbm, col_off_hbm, band_hbm, sub_off_hbm, sub_col_hbm,
    out_ref,
    left, right, rtab, cheb, rphase, cphase, inner, outbox, inbox, vmat, umat,
    wrow_ref, wcol_ref, w_ref, row_off_ref, col_off_ref, band_ref, sub_off_ref, sub_col_ref,
    isem, lsem, osem, ssem, rsem,
):
    n_row, n_col, n_sub, facet, sg, chunks = dims
    r = lax.axis_index("frow")
    c = lax.axis_index("fcol")
    ub, vb = sg // n_row, sg // n_col
    center = facet // 2
    wide = n_col * COL_TERMS
    deep = n_row * ROW_TERMS
    f32, b16 = jnp.float32, jnp.bfloat16

    step = facet // chunks
    images = [
        [
            pltpu.make_async_copy(
                image_hbm.at[i, h * step : (h + 1) * step, :],
                left.at[h * step : (h + 1) * step, i * facet : (i + 1) * facet],
                isem.at[h, i],
            )
            for i in range(2)
        ]
        for h in range(chunks)
    ]
    smalls = [
        pltpu.make_async_copy(src, dst, lsem.at[i])
        for i, (src, dst) in enumerate(
            [
                (sub_col_hbm, sub_col_ref),
                (w_hbm, w_ref),
                (band_hbm, band_ref),
                (sub_off_hbm, sub_off_ref),
                (row_off_hbm, row_off_ref),
                (col_off_hbm, col_off_ref),
                (wrow_hbm, wrow_ref),
                (wcol_hbm, wcol_ref),
            ]
        )
    ]
    for copy in smalls:
        copy.start()
    for pair in images:
        for copy in pair:
            copy.start()

    order = [(dr, dc) for dr in list(range(2, n_row)) + [1, 0] for dc in list(range(1, n_col)) + [0]]
    order = [at for at in order if at != (0, 0)]
    barrier = pltpu.get_barrier_semaphore()
    for dr, dc in order:
        peer = ((r + dr) % n_row, (c + dc) % n_col)
        pl.semaphore_signal(barrier, inc=1, device_id=peer, device_id_type=MESH)

    lane = iota((8, facet), 1)
    local = (lane - center).astype(f32) * (1.0 / center)
    sub = iota((8, facet), 0)
    before, now = jnp.ones_like(local), local
    low = jnp.where(sub == 0, before, now)
    high = low
    for n in range(2, COL_TERMS):
        before, now = now, 2.0 * local * now - before
        if n < 8:
            low = jnp.where(sub == n, now, low)
        else:
            high = jnp.where(sub == n - 8, now, high)
    cheb[0:8, :] = low
    cheb[8:16, :] = high
    for h in range(2):
        part = cheb[HALF * h : HALF * (h + 1), :]
        cheb[16 + 8 * h : 24 + 8 * h, :] = jnp.concatenate([part, part], axis=0)

    for copy in smalls:
        copy.wait()
    columns = [sub_col_ref[k] for k in range(n_sub)]

    def by_sub(index, values):
        out = jnp.full(index.shape, values[0])
        for k in range(1, n_sub):
            out = jnp.where(index == k, values[k], out)
        return out

    waves = [w_ref[columns[k]] * (1.0 / TAU) for k in range(n_sub)]

    def phases(table, coords, n_block, block, firsts, shift, gain):
        row = iota((n_sub * n_block, facet), 0)
        which = row // n_block
        start = by_sub(which, firsts) + ((row + shift) % n_block) * block + block // 2
        turns = by_sub(which, waves) * coord_square(coords) - turn(coords * start)
        re, im = phasor(turns)
        table[0] = re * gain
        table[1] = im * gain

    gcol = col_off_ref[c] + iota((1, facet), 1)
    grow = row_off_ref[r] + iota((1, facet), 1)
    scale = 1.0 / math.sqrt(facet * n_col) / math.sqrt(facet * n_row)
    phases(cphase, gcol, n_col, vb, [band_ref[columns[k]] for k in range(n_sub)], c, wcol_ref[...])
    basis = cheb[0:COL_TERMS, :]
    for k in range(n_sub):
        for p in range(n_col):
            at = k * n_col + p
            re = (cphase[0, at : at + 1, :] * basis).astype(b16)
            im = (cphase[1, at : at + 1, :] * basis).astype(b16)
            top = 2 * wide * k + COL_TERMS * p
            right[top : top + COL_TERMS, :facet] = re
            right[top : top + COL_TERMS, facet:] = -im
            right[top + wide : top + wide + COL_TERMS, :facet] = im
            right[top + wide : top + wide + COL_TERMS, facet:] = re

    phases(rphase, grow, n_row, ub, [sub_off_ref[k] for k in range(n_sub)], 0, wrow_ref[...] * scale)
    first_half = sub < HALF
    for k in range(n_sub):
        for i in range(2):
            for q in range(0, n_row, 4):
                pairs = []
                for b in (q, q + 2):
                    at = k * n_row + b
                    pairs.append(
                        jnp.where(first_half, rphase[i, at : at + 1, :], rphase[i, at + 1 : at + 2, :])
                    )
                for h in range(2):
                    terms = cheb[16 + 8 * h : 24 + 8 * h, :]
                    value = jnp.concatenate([pair * terms for pair in pairs], axis=0).astype(b16)
                    top = i * deep + h * HALF * n_row + HALF * q
                    rtab[k, top : top + 16, :] = value

    for h in range(chunks):
        for copy in images[h]:
            copy.wait()
        rows = slice(h * step, (h + 1) * step)
        inner[rows, :] = lax.dot_general(
            left[rows, :], right[...], (((1,), (1,)), ((), ())), preferred_element_type=f32
        ).astype(b16)

    slot = iota((HALF * n_row, 2 * wide), 1) // COL_TERMS
    half_sign = jnp.where(iota((deep, 2 * wide), 1) < wide, -1.0, 1.0)
    turned = []
    for k in range(n_sub):
        product = jnp.dot(
            rtab[k], inner[:, 2 * wide * k : 2 * wide * (k + 1)], preferred_element_type=f32
        )
        moments = product[:deep] + half_sign * pltpu.roll(product[deep:], wide, 1)
        for h in range(2):
            g = 2 * k + h
            value = moments[HALF * n_row * h : HALF * n_row * (h + 1)]
            turned.append(value if g == 0 else pltpu.roll(value, COL_TERMS * g, 1))
    for d in range(n_col):
        box = turned[0]
        for g in range(1, n_col):
            box = jnp.where(slot % n_col == (d + g) % n_col, turned[g], box)
        outbox[d] = box

    mine = pl.ds(HALF * r, HALF)
    own = pltpu.make_async_copy(outbox.at[0, mine, :], inbox.at[0, mine, :], osem)
    own.start()
    pl.semaphore_wait(barrier, n_row * n_col - 1)
    copies = []
    for to in range(n_row):
        for at in range(n_col):

            @pl.when(jnp.logical_or(r != to, c != at))
            def _():
                pltpu.make_async_remote_copy(
                    src_ref=outbox.at[(at + n_col - c) % n_col, pl.ds(HALF * to, HALF), :],
                    dst_ref=inbox.at[(at + n_col - c) % n_col, mine, :],
                    send_sem=ssem.at[to, at],
                    recv_sem=rsem.at[r, c],
                    device_id=(to, at),
                    device_id_type=MESH,
                ).start()

    for dr, dc in order:
        fr, fc = (r + dr) % n_row, (c + n_col - dc) % n_col
        copies.append(
            pltpu.make_async_remote_copy(
                src_ref=outbox.at[dc, mine, :],
                dst_ref=inbox.at[dc, pl.ds(HALF * fr, HALF), :],
                send_sem=ssem.at[(r + dr) % n_row, (c + dc) % n_col],
                recv_sem=rsem.at[fr, fc],
                device_id=((r + dr) % n_row, (c + dc) % n_col),
                device_id_type=MESH,
            )
        )

    row = iota((wide, vb), 0)
    off = iota((wide, vb), 1) - vb // 2
    which, term = row // COL_TERMS, row % COL_TERMS
    start = jnp.full((wide, vb), center)
    for p in range(n_col):
        start = jnp.where(which == p, col_off_ref[(c + n_col - p) % n_col] + center, start)
    re, im = phasor(-turn(start * off) - 0.25 * (term % 4).astype(f32))
    size = bessel(term, off.astype(f32) * (TAU * center / IMAGE), COL_TERMS)
    re, im = re * size, im * size
    table = jnp.concatenate(
        [jnp.concatenate([re, im], axis=1), jnp.concatenate([-im, re], axis=1)], axis=0
    )
    high_part, low_part = split(table)
    vmat[0 : 2 * wide, :] = high_part
    vmat[2 * wide : 4 * wide, :] = high_part
    vmat[4 * wide : 6 * wide, :] = low_part

    lanes = iota((ub, deep), 1)
    off = iota((ub, deep), 0) - ub // 2
    which = lanes // HALF % n_row
    term = lanes // (HALF * n_row) * HALF + lanes % HALF
    start = jnp.full((ub, deep), center)
    for b in range(n_row):
        start = jnp.where(which == b, row_off_ref[b] + center, start)
    re, im = phasor(-turn(start * off) - 0.25 * (term % 4).astype(f32))
    size = bessel(term, off.astype(f32) * (TAU * center / IMAGE), ROW_TERMS)
    for i, part in enumerate((re * size, im * size)):
        high_part, low_part = split(part)
        rows = slice(i * ub, (i + 1) * ub)
        umat[rows, 0:deep] = high_part
        umat[rows, deep : 2 * deep] = low_part
        umat[rows, 2 * deep : 3 * deep] = high_part

    own.wait()
    for copy in copies:
        copy.wait_recv()

    boxes = [inbox[d] for d in range(n_col)]
    for k in range(n_sub):
        halves = []
        for h in range(2):
            g = 2 * k + h
            value = boxes[0]
            for d in range(1, n_col):
                value = jnp.where(slot % n_col == (d + g) % n_col, boxes[d], value)
            halves.append(value if g == 0 else pltpu.roll(value, 2 * wide - COL_TERMS * g, 1))
        high_part, low_part = split(jnp.concatenate(halves, axis=0))
        x = jnp.dot(
            jnp.concatenate([high_part, low_part, high_part], axis=1),
            vmat[...],
            preferred_element_type=f32,
        )
        high_part, low_part = split(x)
        y = jnp.dot(
            umat[...],
            jnp.concatenate([high_part, high_part, low_part], axis=0),
            preferred_element_type=f32,
        )
        out_ref[k, 0] = y[:ub, :vb] - y[ub:, vb:]
        out_ref[k, 1] = y[:ub, vb:] + y[ub:, :vb]
    for copy in copies:
        copy.wait_send()


def store_kernel(held, out_hbm, sem):
    copy = pltpu.make_async_copy(held, out_hbm, sem)
    copy.start()
    copy.wait()


def fused_local(n_row, n_col, image, *rest):
    facet = image.shape[1]
    n_sub = rest[6].shape[0]
    chunks = 2
    wide, deep = n_col * COL_TERMS, n_row * ROW_TERMS
    ub, vb = SG // n_row, SG // n_col
    f32, b16, i32 = jnp.float32, jnp.bfloat16, jnp.int32
    vmem, smem, dma = pltpu.VMEM, pltpu.SMEM, pltpu.SemaphoreType.DMA
    rest = [rest[0].reshape(1, -1), rest[1].reshape(1, -1), *rest[2:]]
    held = pl.pallas_call(
        functools.partial(fused_kernel, (n_row, n_col, n_sub, facet, SG, chunks)),
        out_shape=vmem((n_sub, 2, ub, vb), f32),
        in_specs=[pl.BlockSpec(memory_space=pl.ANY)] * 9,
        out_specs=pl.BlockSpec(memory_space=vmem),
        scratch_shapes=[
            vmem((facet, 2 * facet), b16),
            vmem((2 * n_sub * wide, 2 * facet), b16),
            vmem((n_sub, 2 * deep, facet), b16),
            vmem((32, facet), f32),
            vmem((2, n_sub * n_row, facet), f32),
            vmem((2, n_sub * n_col, facet), f32),
            vmem((facet, 2 * n_sub * wide), b16),
            vmem((n_col, HALF * n_row, 2 * wide), f32),
            vmem((n_col, HALF * n_row, 2 * wide), f32),
            vmem((6 * wide, 2 * vb), b16),
            vmem((2 * ub, 3 * deep), b16),
            *[vmem(a.shape, a.dtype) for a in rest[:2]],
            *[smem(a.shape, a.dtype) for a in rest[2:]],
            dma((chunks, 2)),
            dma((8,)),
            dma,
            dma((n_row, n_col)),
            dma((n_row, n_col)),
        ],
        compiler_params=pltpu.CompilerParams(
            collective_id=0, has_side_effects=True, vmem_limit_bytes=56 << 20
        ),
    )(image, *rest)
    return held


def solution(mesh):
    n_row, n_col = mesh.shape["frow"], mesh.shape["fcol"]
    ub, vb = SG // n_row, SG // n_col

    def local(image, *rest):
        facet, n_sub = image.shape[1], rest[-1].shape[0]
        tiled = (
            SG == ub * n_row == vb * n_col
            and n_row % 4 == 0
            and n_col == 2 * n_sub
            and n_col * COL_TERMS == 64
            and ub % 8 == 0
            and vb % 128 == 0
            and image.shape[2] == facet
            and facet % 256 == 0
            and remainder(facet // 2, ub // 2, ROW_TERMS) < 2.0**-24
            and remainder(facet // 2, vb // 2, COL_TERMS) < 2.0**-24
        )
        return (functools.partial(fused_local, n_row, n_col) if tiled else general_local)(image, *rest)

    placed = (P(None, "frow", "fcol"), P("frow"), P("fcol"), P(), P(), P(), P(), P(), P())
    return jax.shard_map(
        local, mesh=mesh, in_specs=placed, out_specs=P(None, None, "frow", "fcol"), check_vma=False
    )
```

```python
import functools
import math

import jax
import jax.numpy as jnp
from jax import lax
from jax.experimental import pallas as pl
from jax.experimental.pallas import tpu as pltpu
from jax.sharding import PartitionSpec as P

SG = 512
IMAGE = 65536


def phase_index(first, second):
    high = first * (second // 256) % 256 * 256
    return (high + first * (second % 256)) % 65536


def dft_table(coords, freqs):
    angle = phase_index(coords, freqs).astype(jnp.float32) * (2.0 * math.pi / IMAGE)
    return (jnp.cos(angle).astype(jnp.bfloat16), (-jnp.sin(angle)).astype(jnp.bfloat16))


def coord_unit(coords):
    return (coords % IMAGE).astype(jnp.float32) / IMAGE - 0.5


def block_table(table_re, table_im):
    upper = jnp.concatenate([table_re, table_im], axis=1)
    lower = jnp.concatenate([-table_im, table_re], axis=1)
    return jnp.concatenate([upper, lower], axis=0)


def general_local(
    image,
    window_rows,
    window_cols,
    w_terms,
    facet_row_offset,
    facet_col_offset,
    band_offset,
    sub_row_offset,
    sub_column,
):
    facet = image.shape[1]
    column_count = band_offset.shape[0]
    sub_count = sub_row_offset.shape[0]
    frow_index = lax.axis_index("frow")
    fcol_index = lax.axis_index("fcol")
    freq_base = jnp.arange(SG, dtype=jnp.int32)
    gcol = facet_col_offset[fcol_index] + jnp.arange(image.shape[2], dtype=jnp.int32)
    mcoord = coord_unit(gcol)
    row_base = facet_row_offset[frow_index]
    row_ids = row_base + jnp.arange(facet, dtype=jnp.int32)
    radius = coord_unit(row_ids)[:, None] ** 2 + mcoord[None, :] ** 2
    scale = window_rows[:, None] * window_cols[None, :]
    first = image[0].astype(jnp.float32) * scale
    second = image[1].astype(jnp.float32) * scale
    prepared = []
    for column in range(column_count):
        angle = w_terms[column] * radius
        cosine = jnp.cos(angle)
        sine = jnp.sin(angle)
        prep_re = (first * cosine - second * sine).astype(jnp.bfloat16)
        prep_im = (first * sine + second * cosine).astype(jnp.bfloat16)
        prepared.append(jnp.concatenate([prep_re, prep_im], axis=1))
    band_dev = SG // lax.axis_size("fcol")
    freqs = jnp.arange(band_dev * lax.axis_size("fcol"), dtype=jnp.int32)
    outputs = []
    for column in range(column_count):
        table_re, table_im = dft_table(gcol[:, None], band_offset[column] + freqs[None, :])
        whole_table = block_table(table_re, table_im)
        product = lax.dot_general(
            whole_table,
            prepared[column],
            (((0,), (1,)), ((), ())),
            preferred_element_type=jnp.float32,
        )
        outputs.append(
            product.reshape(2, band_dev * lax.axis_size("fcol"), facet).transpose(1, 0, 2)
        )
    summed = lax.psum_scatter(jnp.stack(outputs, axis=1), "fcol", scatter_dimension=0, tiled=True)
    banded = (summed / math.sqrt(facet * lax.axis_size("fcol"))).astype(jnp.bfloat16)
    chosen = jnp.take(banded, sub_column, axis=1)
    right_side = chosen.transpose(1, 2, 3, 0).reshape(sub_count, 2 * facet, band_dev)
    table_re, table_im = dft_table(
        row_ids[None, :, None], sub_row_offset[:, None, None] + freq_base[None, None, :]
    )
    left_real = jnp.concatenate([table_re, -table_im], axis=1)
    left_imag = jnp.concatenate([table_im, table_re], axis=1)
    left_side = jnp.stack([left_real, left_imag], axis=2)
    term = jnp.einsum("kxcu,kxv->kcuv", left_side, right_side, preferred_element_type=jnp.float32)
    term = term * (1.0 / math.sqrt(facet * lax.axis_size("frow")))
    return lax.psum_scatter(term, "frow", scatter_dimension=2, tiled=True)


MESH = pl.DeviceIdType.MESH
TAU = 2.0 * math.pi
ROW_TERMS = 8
COL_TERMS = 16
HALF = ROW_TERMS // 2
BESSEL_STEPS = 8


def remainder(half_facet, half_block, terms):
    z_max = TAU * half_facet * half_block / IMAGE
    return 2.0 * (z_max / 2.0) ** terms / math.factorial(terms)


def iota(shape, axis):
    return lax.broadcasted_iota(jnp.int32, shape, axis)


def turn(index):
    return (index & (IMAGE - 1)).astype(jnp.float32) * (1.0 / IMAGE)


def phasor(turns):
    quadrant = jnp.floor(turns * 4.0 + 0.5)
    t = (turns - quadrant * 0.25) * TAU
    s = t * t
    sine = t * (1.0 + s * (-1 / 6 + s * (1 / 120 + s * (-1 / 5040 + s * (1 / 362880)))))
    cosine = 1.0 + s * (-1 / 2 + s * (1 / 24 + s * (-1 / 720 + s * (1 / 40320 + s * (-1 / 3628800)))))
    q = quadrant.astype(jnp.int32)
    odd = (q & 1) == 1
    real = jnp.where(odd, sine, cosine)
    imag = jnp.where(odd, cosine, sine)
    real = jnp.where(((q + 1) & 2) == 2, -real, real)
    imag = jnp.where((q & 2) == 2, -imag, imag)
    return real, imag


def coord_square(coords):
    unit = (coords & (IMAGE - 1)).astype(jnp.float32) * (1.0 / IMAGE) - 0.5
    return unit * unit


def bessel(order, z, terms):
    half = z * 0.5
    q = half * half
    lead = jnp.where(order == 0, 1.0, 2.0)
    for i in range(1, terms):
        lead = jnp.where(order >= i, lead * half * (1.0 / i), lead)
    tail = jnp.ones_like(z)
    for j in range(BESSEL_STEPS, 0, -1):
        tail = 1.0 - tail * q / (j * (order + j)).astype(jnp.float32)
    return lead * tail


def split(value):
    high = value.astype(jnp.bfloat16)
    return high, (value - high.astype(jnp.float32)).astype(jnp.bfloat16)


def fused_kernel(
    dims,
    image_hbm, wrow_hbm, wcol_hbm, w_hbm, row_off_hbm, col_off_hbm, band_hbm, sub_off_hbm, sub_col_hbm,
    out_ref,
    left, right, rtab, cheb, rphase, cphase, inner, outbox, inbox, vmat, umat,
    wrow_ref, wcol_ref, w_ref, row_off_ref, col_off_ref, band_ref, sub_off_ref, sub_col_ref,
    isem, lsem, ssem, rsem,
):
    n_row, n_col, n_sub, facet, sg, chunks = dims
    r = lax.axis_index("frow")
    c = lax.axis_index("fcol")
    ub, vb = sg // n_row, sg // n_col
    center = facet // 2
    wide = n_col * COL_TERMS
    deep = n_row * ROW_TERMS
    tall = HALF * n_row
    f32, b16 = jnp.float32, jnp.bfloat16

    step = facet // chunks
    images = [
        [
            pltpu.make_async_copy(
                image_hbm.at[i, h * step : (h + 1) * step, :],
                left.at[h * step : (h + 1) * step, i * facet : (i + 1) * facet],
                isem.at[h, i],
            )
            for i in range(2)
        ]
        for h in range(chunks)
    ]
    smalls = [
        pltpu.make_async_copy(src, dst, lsem.at[i])
        for i, (src, dst) in enumerate(
            [
                (sub_col_hbm, sub_col_ref),
                (w_hbm, w_ref),
                (band_hbm, band_ref),
                (sub_off_hbm, sub_off_ref),
                (row_off_hbm, row_off_ref),
                (col_off_hbm, col_off_ref),
                (wrow_hbm, wrow_ref),
                (wcol_hbm, wcol_ref),
            ]
        )
    ]
    for copy in smalls:
        copy.start()
    for pair in images:
        for copy in pair:
            copy.start()

    order = [(dr, dc) for dr in list(range(2, n_row)) + [1, 0] for dc in list(range(1, n_col)) + [0]]
    order = [at for at in order if at != (0, 0)]
    barrier = pltpu.get_barrier_semaphore()
    for dr, dc in order:
        peer = ((r + dr) % n_row, (c + dc) % n_col)
        pl.semaphore_signal(barrier, inc=1, device_id=peer, device_id_type=MESH)

    lane = iota((8, facet), 1)
    local = (lane - center).astype(f32) * (1.0 / center)
    sub = iota((8, facet), 0)
    before, now = jnp.ones_like(local), local
    low = jnp.where(sub == 0, before, now)
    high = low
    for n in range(2, COL_TERMS):
        before, now = now, 2.0 * local * now - before
        if n < 8:
            low = jnp.where(sub == n, now, low)
        else:
            high = jnp.where(sub == n - 8, now, high)
    cheb[0:8, :] = low
    cheb[8:16, :] = high
    for h in range(2):
        part = cheb[HALF * h : HALF * (h + 1), :]
        cheb[16 + 8 * h : 24 + 8 * h, :] = jnp.concatenate([part, part], axis=0)

    for copy in smalls:
        copy.wait()
    columns = [sub_col_ref[k] for k in range(n_sub)]

    def by_sub(index, values):
        out = jnp.full(index.shape, values[0])
        for k in range(1, n_sub):
            out = jnp.where(index == k, values[k], out)
        return out

    waves = [w_ref[columns[k]] * (1.0 / TAU) for k in range(n_sub)]

    def phases(table, coords, n_block, block, firsts, shift, gain):
        row = iota((n_sub * n_block, facet), 0)
        which = row // n_block
        start = by_sub(which, firsts) + ((row + shift) % n_block) * block + block // 2
        turns = by_sub(which, waves) * coord_square(coords) - turn(coords * start)
        re, im = phasor(turns)
        table[0] = re * gain
        table[1] = im * gain

    gcol = col_off_ref[c] + iota((1, facet), 1)
    grow = row_off_ref[r] + iota((1, facet), 1)
    scale = 1.0 / math.sqrt(facet * n_col) / math.sqrt(facet * n_row)
    phases(cphase, gcol, n_col, vb, [band_ref[columns[k]] for k in range(n_sub)], c, wcol_ref[...])
    basis = cheb[0:COL_TERMS, :]
    for k in range(n_sub):
        for p in range(n_col):
            at = k * n_col + p
            re = (cphase[0, at : at + 1, :] * basis).astype(b16)
            im = (cphase[1, at : at + 1, :] * basis).astype(b16)
            top = 2 * wide * k + COL_TERMS * p
            right[top : top + COL_TERMS, :facet] = re
            right[top : top + COL_TERMS, facet:] = -im
            right[top + wide : top + wide + COL_TERMS, :facet] = im
            right[top + wide : top + wide + COL_TERMS, facet:] = re

    phases(rphase, grow, n_row, ub, [sub_off_ref[k] for k in range(n_sub)], 0, wrow_ref[...] * scale)
    first_half = sub < HALF
    for k in range(n_sub):
        for i in range(2):
            for q in range(0, n_row, 4):
                pairs = []
                for b in (q, q + 2):
                    at = k * n_row + b
                    pairs.append(
                        jnp.where(first_half, rphase[i, at : at + 1, :], rphase[i, at + 1 : at + 2, :])
                    )
                for h in range(2):
                    terms = cheb[16 + 8 * h : 24 + 8 * h, :]
                    value = jnp.concatenate([pair * terms for pair in pairs], axis=0).astype(b16)
                    top = i * deep + h * HALF * n_row + HALF * q
                    rtab[k, top : top + 16, :] = value

    for h in range(chunks):
        for copy in images[h]:
            copy.wait()
        rows = slice(h * step, (h + 1) * step)
        inner[rows, :] = lax.dot_general(
            left[rows, :], right[...], (((1,), (1,)), ((), ())), preferred_element_type=f32
        ).astype(b16)

    slot = iota((tall, 2 * wide), 1) // COL_TERMS
    product = jnp.dot(
        rtab[...].reshape(2 * n_sub * deep, facet), inner[...], preferred_element_type=f32
    )
    turned = []
    for g in range(2 * n_sub):
        k, h = g // 2, g % 2
        lanes = slice(2 * wide * k, 2 * wide * (k + 1))
        top = 2 * deep * k + tall * h
        first = product[top : top + tall, lanes]
        second = product[top + deep : top + deep + tall, lanes]
        if g > 0:
            first = pltpu.roll(first, COL_TERMS * g, 1)
        second = pltpu.roll(second, (wide + COL_TERMS * g) % (2 * wide), 1)
        real = (slot - g) % (2 * n_col) < n_col
        turned.append(first + jnp.where(real, -second, second))
    for d in range(n_col):
        box = turned[0]
        for g in range(1, n_col):
            box = jnp.where(slot % n_col == (d + g) % n_col, turned[g], box)
        outbox[tall * d : tall * (d + 1), :] = box

    def rows_of(d, i):
        return pl.ds(tall * d + HALF * i, HALF)

    pltpu.make_async_copy(outbox.at[rows_of(0, r), :], inbox.at[rows_of(0, r), :], rsem).start()
    pl.semaphore_wait(barrier, n_row * n_col - 1)
    for to in range(n_row):
        for at in range(n_col):

            @pl.when(jnp.logical_or(r != to, c != at))
            def _():
                d = (at + n_col - c) % n_col
                pltpu.make_async_remote_copy(
                    src_ref=outbox.at[rows_of(d, to), :],
                    dst_ref=inbox.at[rows_of(d, r), :],
                    send_sem=ssem,
                    recv_sem=rsem,
                    device_id=(to, at),
                    device_id_type=MESH,
                ).start()

    row = iota((wide, vb), 0)
    off = iota((wide, vb), 1) - vb // 2
    which, term = row // COL_TERMS, row % COL_TERMS
    start = jnp.full((wide, vb), center)
    for p in range(n_col):
        start = jnp.where(which == p, col_off_ref[(c + n_col - p) % n_col] + center, start)
    re, im = phasor(-turn(start * off) - 0.25 * (term % 4).astype(f32))
    size = bessel(term, off.astype(f32) * (TAU * center / IMAGE), COL_TERMS)
    re, im = re * size, im * size
    table = jnp.concatenate(
        [jnp.concatenate([re, im], axis=1), jnp.concatenate([-im, re], axis=1)], axis=0
    )
    high_part, low_part = split(table)
    vmat[0 : 2 * wide, :] = high_part
    vmat[2 * wide : 4 * wide, :] = high_part
    vmat[4 * wide : 6 * wide, :] = low_part

    lanes = iota((ub, deep), 1)
    off = iota((ub, deep), 0) - ub // 2
    which = lanes // HALF % n_row
    term = lanes // (HALF * n_row) * HALF + lanes % HALF
    start = jnp.full((ub, deep), center)
    for b in range(n_row):
        start = jnp.where(which == b, row_off_ref[b] + center, start)
    re, im = phasor(-turn(start * off) - 0.25 * (term % 4).astype(f32))
    size = bessel(term, off.astype(f32) * (TAU * center / IMAGE), ROW_TERMS)
    for i, part in enumerate((re * size, im * size)):
        high_part, low_part = split(part)
        rows = slice(i * ub, (i + 1) * ub)
        umat[rows, 0:deep] = high_part
        umat[rows, deep : 2 * deep] = low_part
        umat[rows, 2 * deep : 3 * deep] = high_part

    pltpu.make_async_copy(inbox, inbox, rsem).wait()

    boxes = [inbox[tall * d : tall * (d + 1), :] for d in range(n_col)]
    halves = []
    for g in range(2 * n_sub):
        value = boxes[0]
        for d in range(1, n_col):
            value = jnp.where(slot % n_col == (d + g) % n_col, boxes[d], value)
        halves.append(value if g == 0 else pltpu.roll(value, 2 * wide - COL_TERMS * g, 1))
    high_part, low_part = split(jnp.concatenate(halves, axis=0))
    x = jnp.dot(
        jnp.concatenate([high_part, low_part, high_part], axis=1),
        vmat[...],
        preferred_element_type=f32,
    )
    for k in range(n_sub):
        high_part, low_part = split(x[deep * k : deep * (k + 1)])
        y = jnp.dot(
            umat[...],
            jnp.concatenate([high_part, high_part, low_part], axis=0),
            preferred_element_type=f32,
        )
        out_ref[k, 0] = y[:ub, :vb] - y[ub:, vb:]
        out_ref[k, 1] = y[:ub, vb:] + y[ub:, :vb]
    sent = outbox.at[0 : HALF * (n_row * n_col - 1), :]
    pltpu.make_async_copy(sent, sent, ssem).wait()


def fused_local(n_row, n_col, image, *rest):
    facet = image.shape[1]
    n_sub = rest[6].shape[0]
    chunks = 1
    wide, deep = n_col * COL_TERMS, n_row * ROW_TERMS
    ub, vb = SG // n_row, SG // n_col
    f32, b16, i32 = jnp.float32, jnp.bfloat16, jnp.int32
    vmem, smem, dma = pltpu.VMEM, pltpu.SMEM, pltpu.SemaphoreType.DMA
    rest = [rest[0].reshape(1, -1), rest[1].reshape(1, -1), *rest[2:]]
    held = pl.pallas_call(
        functools.partial(fused_kernel, (n_row, n_col, n_sub, facet, SG, chunks)),
        out_shape=vmem((n_sub, 2, ub, vb), f32),
        in_specs=[pl.BlockSpec(memory_space=pl.ANY)] * 9,
        out_specs=pl.BlockSpec(memory_space=vmem),
        scratch_shapes=[
            vmem((facet, 2 * facet), b16),
            vmem((2 * n_sub * wide, 2 * facet), b16),
            vmem((n_sub, 2 * deep, facet), b16),
            vmem((32, facet), f32),
            vmem((2, n_sub * n_row, facet), f32),
            vmem((2, n_sub * n_col, facet), f32),
            vmem((facet, 2 * n_sub * wide), b16),
            vmem((n_col * HALF * n_row, 2 * wide), f32),
            vmem((n_col * HALF * n_row, 2 * wide), f32),
            vmem((6 * wide, 2 * vb), b16),
            vmem((2 * ub, 3 * deep), b16),
            *[vmem(a.shape, a.dtype) for a in rest[:2]],
            *[smem(a.shape, a.dtype) for a in rest[2:]],
            dma((chunks, 2)),
            dma((8,)),
            dma,
            dma,
        ],
        compiler_params=pltpu.CompilerParams(
            collective_id=0, has_side_effects=True, vmem_limit_bytes=56 << 20
        ),
    )(image, *rest)
    return held


def solution(mesh):
    n_row, n_col = mesh.shape["frow"], mesh.shape["fcol"]
    ub, vb = SG // n_row, SG // n_col

    def local(image, *rest):
        facet, n_sub = image.shape[1], rest[-1].shape[0]
        tiled = (
            SG == ub * n_row == vb * n_col
            and n_row % 4 == 0
            and n_col == 2 * n_sub
            and n_col * COL_TERMS == 64
            and ub % 8 == 0
            and vb % 128 == 0
            and image.shape[2] == facet
            and facet % 256 == 0
            and remainder(facet // 2, ub // 2, ROW_TERMS) < 2.0**-24
            and remainder(facet // 2, vb // 2, COL_TERMS) < 2.0**-24
        )
        return (functools.partial(fused_local, n_row, n_col) if tiled else general_local)(image, *rest)

    placed = (P(None, "frow", "fcol"), P("frow"), P("fcol"), P(), P(), P(), P(), P(), P())
    return jax.shard_map(
        local, mesh=mesh, in_specs=placed, out_specs=P(None, None, "frow", "fcol"), check_vma=False
    )
```

```python
import functools
import math

import jax
import jax.numpy as jnp
from jax import lax
from jax.experimental import pallas as pl
from jax.experimental.pallas import tpu as pltpu
from jax.sharding import PartitionSpec as P

SG = 512
IMAGE = 65536


def phase_index(first, second):
    high = first * (second // 256) % 256 * 256
    return (high + first * (second % 256)) % 65536


def dft_table(coords, freqs):
    angle = phase_index(coords, freqs).astype(jnp.float32) * (2.0 * math.pi / IMAGE)
    return (jnp.cos(angle).astype(jnp.bfloat16), (-jnp.sin(angle)).astype(jnp.bfloat16))


def coord_unit(coords):
    return (coords % IMAGE).astype(jnp.float32) / IMAGE - 0.5


def block_table(table_re, table_im):
    upper = jnp.concatenate([table_re, table_im], axis=1)
    lower = jnp.concatenate([-table_im, table_re], axis=1)
    return jnp.concatenate([upper, lower], axis=0)


def general_local(
    image,
    window_rows,
    window_cols,
    w_terms,
    facet_row_offset,
    facet_col_offset,
    band_offset,
    sub_row_offset,
    sub_column,
):
    facet = image.shape[1]
    column_count = band_offset.shape[0]
    sub_count = sub_row_offset.shape[0]
    frow_index = lax.axis_index("frow")
    fcol_index = lax.axis_index("fcol")
    freq_base = jnp.arange(SG, dtype=jnp.int32)
    gcol = facet_col_offset[fcol_index] + jnp.arange(image.shape[2], dtype=jnp.int32)
    mcoord = coord_unit(gcol)
    row_base = facet_row_offset[frow_index]
    row_ids = row_base + jnp.arange(facet, dtype=jnp.int32)
    radius = coord_unit(row_ids)[:, None] ** 2 + mcoord[None, :] ** 2
    scale = window_rows[:, None] * window_cols[None, :]
    first = image[0].astype(jnp.float32) * scale
    second = image[1].astype(jnp.float32) * scale
    prepared = []
    for column in range(column_count):
        angle = w_terms[column] * radius
        cosine = jnp.cos(angle)
        sine = jnp.sin(angle)
        prep_re = (first * cosine - second * sine).astype(jnp.bfloat16)
        prep_im = (first * sine + second * cosine).astype(jnp.bfloat16)
        prepared.append(jnp.concatenate([prep_re, prep_im], axis=1))
    band_dev = SG // lax.axis_size("fcol")
    freqs = jnp.arange(band_dev * lax.axis_size("fcol"), dtype=jnp.int32)
    outputs = []
    for column in range(column_count):
        table_re, table_im = dft_table(gcol[:, None], band_offset[column] + freqs[None, :])
        whole_table = block_table(table_re, table_im)
        product = lax.dot_general(
            whole_table,
            prepared[column],
            (((0,), (1,)), ((), ())),
            preferred_element_type=jnp.float32,
        )
        outputs.append(
            product.reshape(2, band_dev * lax.axis_size("fcol"), facet).transpose(1, 0, 2)
        )
    summed = lax.psum_scatter(jnp.stack(outputs, axis=1), "fcol", scatter_dimension=0, tiled=True)
    banded = (summed / math.sqrt(facet * lax.axis_size("fcol"))).astype(jnp.bfloat16)
    chosen = jnp.take(banded, sub_column, axis=1)
    right_side = chosen.transpose(1, 2, 3, 0).reshape(sub_count, 2 * facet, band_dev)
    table_re, table_im = dft_table(
        row_ids[None, :, None], sub_row_offset[:, None, None] + freq_base[None, None, :]
    )
    left_real = jnp.concatenate([table_re, -table_im], axis=1)
    left_imag = jnp.concatenate([table_im, table_re], axis=1)
    left_side = jnp.stack([left_real, left_imag], axis=2)
    term = jnp.einsum("kxcu,kxv->kcuv", left_side, right_side, preferred_element_type=jnp.float32)
    term = term * (1.0 / math.sqrt(facet * lax.axis_size("frow")))
    return lax.psum_scatter(term, "frow", scatter_dimension=2, tiled=True)


MESH = pl.DeviceIdType.MESH
TAU = 2.0 * math.pi
ROW_TERMS = 8
COL_TERMS = 16
HALF = ROW_TERMS // 2
BESSEL_STEPS = 8
MXU = 256


def remainder(half_facet, half_block, terms):
    z_max = TAU * half_facet * half_block / IMAGE
    return 2.0 * (z_max / 2.0) ** terms / math.factorial(terms)


def iota(shape, axis):
    return lax.broadcasted_iota(jnp.int32, shape, axis)


def turn(index):
    return (index & (IMAGE - 1)).astype(jnp.float32) * (1.0 / IMAGE)


def phasor(turns):
    quadrant = jnp.floor(turns * 4.0 + 0.5)
    t = (turns - quadrant * 0.25) * TAU
    s = t * t
    sine = t * (1.0 + s * (-1 / 6 + s * (1 / 120 + s * (-1 / 5040 + s * (1 / 362880)))))
    cosine = 1.0 + s * (-1 / 2 + s * (1 / 24 + s * (-1 / 720 + s * (1 / 40320 + s * (-1 / 3628800)))))
    q = quadrant.astype(jnp.int32)
    odd = (q & 1) == 1
    real = jnp.where(odd, sine, cosine)
    imag = jnp.where(odd, cosine, sine)
    real = jnp.where(((q + 1) & 2) == 2, -real, real)
    imag = jnp.where((q & 2) == 2, -imag, imag)
    return real, imag


def coord_square(coords):
    unit = (coords & (IMAGE - 1)).astype(jnp.float32) * (1.0 / IMAGE) - 0.5
    return unit * unit


def bessel(order, z, terms):
    half = z * 0.5
    q = half * half
    lead = jnp.where(order == 0, 1.0, 2.0)
    for i in range(1, terms):
        lead = jnp.where(order >= i, lead * half * (1.0 / i), lead)
    tail = jnp.ones_like(z)
    for j in range(BESSEL_STEPS, 0, -1):
        tail = 1.0 - tail * q / (j * (order + j)).astype(jnp.float32)
    return lead * tail


def split(value):
    high = value.astype(jnp.bfloat16)
    return high, (value - high.astype(jnp.float32)).astype(jnp.bfloat16)


def fused_kernel(
    dims,
    image_hbm, wrow_hbm, wcol_hbm, w_hbm, row_off_hbm, col_off_hbm, band_hbm, sub_off_hbm, sub_col_hbm,
    out_ref,
    left, right, rtab, cheb, rphase, cphase, inner, outbox, inbox, vmat, umat,
    wrow_ref, wcol_ref, w_ref, row_off_ref, col_off_ref, band_ref, sub_off_ref, sub_col_ref,
    isem, lsem, ssem, rsem,
):
    n_row, n_col, n_sub, facet, sg = dims
    r = lax.axis_index("frow")
    c = lax.axis_index("fcol")
    ub, vb = sg // n_row, sg // n_col
    center = facet // 2
    wide = n_col * COL_TERMS
    deep = n_row * ROW_TERMS
    tall = HALF * n_row
    f32, b16 = jnp.float32, jnp.bfloat16

    images = [
        pltpu.make_async_copy(image_hbm.at[i], left.at[:, i * facet : (i + 1) * facet], isem.at[i])
        for i in range(2)
    ]
    smalls = [
        pltpu.make_async_copy(src, dst, lsem.at[i])
        for i, (src, dst) in enumerate(
            [
                (sub_col_hbm, sub_col_ref),
                (w_hbm, w_ref),
                (band_hbm, band_ref),
                (sub_off_hbm, sub_off_ref),
                (row_off_hbm, row_off_ref),
                (col_off_hbm, col_off_ref),
                (wrow_hbm, wrow_ref),
                (wcol_hbm, wcol_ref),
            ]
        )
    ]
    for copy in smalls:
        copy.start()
    for copy in images:
        copy.start()

    order = [(dr, dc) for dr in list(range(2, n_row)) + [1, 0] for dc in list(range(1, n_col)) + [0]]
    order = [at for at in order if at != (0, 0)]
    barrier = pltpu.get_barrier_semaphore()
    for dr, dc in order:
        peer = ((r + dr) % n_row, (c + dc) % n_col)
        pl.semaphore_signal(barrier, inc=1, device_id=peer, device_id_type=MESH)

    lane = iota((8, facet), 1)
    local = (lane - center).astype(f32) * (1.0 / center)
    sub = iota((8, facet), 0)
    before, now = jnp.ones_like(local), local
    low = jnp.where(sub == 0, before, now)
    high = low
    for n in range(2, COL_TERMS):
        before, now = now, 2.0 * local * now - before
        if n < 8:
            low = jnp.where(sub == n, now, low)
        else:
            high = jnp.where(sub == n - 8, now, high)
    cheb[0:8, :] = low
    cheb[8:16, :] = high
    for h in range(2):
        part = cheb[HALF * h : HALF * (h + 1), :]
        cheb[16 + 8 * h : 24 + 8 * h, :] = jnp.concatenate([part, part], axis=0)

    for copy in smalls:
        copy.wait()
    columns = [sub_col_ref[k] for k in range(n_sub)]

    def by_sub(index, values):
        out = jnp.full(index.shape, values[0])
        for k in range(1, n_sub):
            out = jnp.where(index == k, values[k], out)
        return out

    waves = [w_ref[columns[k]] * (1.0 / TAU) for k in range(n_sub)]

    def phases(table, coords, n_block, block, firsts, shift, gain):
        row = iota((n_sub * n_block, facet), 0)
        which = row // n_block
        start = by_sub(which, firsts) + ((row + shift) % n_block) * block + block // 2
        turns = by_sub(which, waves) * coord_square(coords) - turn(coords * start)
        re, im = phasor(turns)
        table[0] = re * gain
        table[1] = im * gain

    gcol = col_off_ref[c] + iota((1, facet), 1)
    grow = row_off_ref[r] + iota((1, facet), 1)
    scale = 1.0 / math.sqrt(facet * n_col) / math.sqrt(facet * n_row)
    phases(cphase, gcol, n_col, vb, [band_ref[columns[k]] for k in range(n_sub)], c, wcol_ref[...])
    basis = cheb[0:COL_TERMS, :]
    for k in range(n_sub):
        for p in range(n_col):
            at = k * n_col + p
            re = (cphase[0, at : at + 1, :] * basis).astype(b16)
            im = (cphase[1, at : at + 1, :] * basis).astype(b16)
            top = 2 * wide * k + COL_TERMS * p
            right[top : top + COL_TERMS, :facet] = re
            right[top : top + COL_TERMS, facet:] = -im
            right[top + wide : top + wide + COL_TERMS, :facet] = im
            right[top + wide : top + wide + COL_TERMS, facet:] = re

    slot = iota((tall, 2 * wide), 1) // COL_TERMS

    def moments(*accs):
        accs = [accs[:2], accs[2:]]
        tiles, per_part = 2 * facet // MXU, facet // MXU

        def push(t):
            for unit in range(2):
                pltpu.matmul_push_rhs(right[:, MXU * t : MXU * (t + 1)], t % 2, unit, transpose=True)

        push(0)
        for t in range(tiles):
            if t % per_part == 0:
                images[t // per_part].wait()
            if t + 1 < tiles:
                push(t + 1)
            for unit in range(2):
                for i in range(2):
                    top = (2 * unit + i) * (facet // 4)
                    pltpu.matmul_acc_lhs(
                        accs[unit][i],
                        left[top : top + facet // 4, MXU * t : MXU * (t + 1)],
                        load_staged_rhs=t % 2 if i == 0 else None,
                    )

        phases(rphase, grow, n_row, ub, [sub_off_ref[k] for k in range(n_sub)], 0, wrow_ref[...] * scale)
        first_half = sub < HALF
        for k in range(n_sub):
            for i in range(2):
                for q in range(0, n_row, 4):
                    pairs = []
                    for b in (q, q + 2):
                        at = k * n_row + b
                        pairs.append(
                            jnp.where(first_half, rphase[i, at : at + 1, :], rphase[i, at + 1 : at + 2, :])
                        )
                    for h in range(2):
                        terms = cheb[16 + 8 * h : 24 + 8 * h, :]
                        value = jnp.concatenate([pair * terms for pair in pairs], axis=0).astype(b16)
                        top = i * deep + h * HALF * n_row + HALF * q
                        rtab[k, top : top + 16, :] = value


        for i in range(2):
            for unit in range(2):
                top = (2 * unit + i) * (facet // 4)
                inner[top : top + facet // 4, :] = pltpu.matmul_pop(accs[unit][i]).astype(b16)

        for unit in range(2):
            pltpu.matmul_push_rhs(inner[MXU * unit : MXU * (unit + 1), :], 0, unit)
        for k in range(n_sub):
            for unit in range(2):
                pltpu.matmul_acc_lhs(
                    accs[unit][k],
                    rtab[k, :, MXU * unit : MXU * (unit + 1)],
                    load_staged_rhs=0 if k == 0 else None,
                )
        turned = []
        for k in range(n_sub):
            lanes = slice(2 * wide * k, 2 * wide * (k + 1))
            product = (pltpu.matmul_pop(accs[0][k]) + pltpu.matmul_pop(accs[1][k]))[:, lanes]
            for h in range(2):
                g = 2 * k + h
                first = product[tall * h : tall * (h + 1)]
                second = product[deep + tall * h : deep + tall * (h + 1)]
                if g > 0:
                    first = pltpu.roll(first, COL_TERMS * g, 1)
                second = pltpu.roll(second, (wide + COL_TERMS * g) % (2 * wide), 1)
                real = (slot - g) % (2 * n_col) < n_col
                turned.append(first + jnp.where(real, -second, second))
        for d in range(n_col):
            box = turned[0]
            for g in range(1, n_col):
                box = jnp.where(slot % n_col == (d + g) % n_col, turned[g], box)
            outbox[tall * d : tall * (d + 1), :] = box

    pl.run_scoped(
        moments, *[pltpu.ACC(unit)((facet // 4, MXU), f32) for unit in (0, 0, 1, 1)]
    )

    def rows_of(d, i):
        return pl.ds(tall * d + HALF * i, HALF)

    pltpu.make_async_copy(outbox.at[rows_of(0, r), :], inbox.at[rows_of(0, r), :], rsem).start()
    pl.semaphore_wait(barrier, n_row * n_col - 1)
    for to in range(n_row):
        for at in range(n_col):

            @pl.when(jnp.logical_or(r != to, c != at))
            def _():
                d = (at + n_col - c) % n_col
                pltpu.make_async_remote_copy(
                    src_ref=outbox.at[rows_of(d, to), :],
                    dst_ref=inbox.at[rows_of(d, r), :],
                    send_sem=ssem,
                    recv_sem=rsem,
                    device_id=(to, at),
                    device_id_type=MESH,
                ).start()

    row = iota((wide, vb), 0)
    off = iota((wide, vb), 1) - vb // 2
    which, term = row // COL_TERMS, row % COL_TERMS
    start = jnp.full((wide, vb), center)
    for p in range(n_col):
        start = jnp.where(which == p, col_off_ref[(c + n_col - p) % n_col] + center, start)
    re, im = phasor(-turn(start * off) - 0.25 * (term % 4).astype(f32))
    size = bessel(term, off.astype(f32) * (TAU * center / IMAGE), COL_TERMS)
    re, im = re * size, im * size
    table = jnp.concatenate(
        [jnp.concatenate([re, im], axis=1), jnp.concatenate([-im, re], axis=1)], axis=0
    )
    high_part, low_part = split(table)
    for i, part in enumerate((high_part, high_part, low_part, low_part)):
        vmat[2 * wide * i : 2 * wide * (i + 1), :] = part

    lanes = iota((ub, deep), 1)
    off = iota((ub, deep), 0) - ub // 2
    which = lanes // HALF % n_row
    term = lanes // (HALF * n_row) * HALF + lanes % HALF
    start = jnp.full((ub, deep), center)
    for b in range(n_row):
        start = jnp.where(which == b, row_off_ref[b] + center, start)
    re, im = phasor(-turn(start * off) - 0.25 * (term % 4).astype(f32))
    size = bessel(term, off.astype(f32) * (TAU * center / IMAGE), ROW_TERMS)
    for i, part in enumerate((re * size, im * size)):
        high_part, low_part = split(part)
        rows = slice(i * ub, (i + 1) * ub)
        for j, piece in enumerate((high_part, high_part, low_part, low_part)):
            umat[rows, deep * j : deep * (j + 1)] = piece

    def subgrids(*accs):
        for unit in range(2):
            pltpu.matmul_push_rhs(vmat[MXU * unit : MXU * (unit + 1), :], 0, unit)
        pltpu.make_async_copy(inbox, inbox, rsem).wait()
        boxes = [inbox[tall * d : tall * (d + 1), :] for d in range(n_col)]
        halves = []
        for g in range(2 * n_sub):
            value = boxes[0]
            for d in range(1, n_col):
                value = jnp.where(slot % n_col == (d + g) % n_col, boxes[d], value)
            halves.append(value if g == 0 else pltpu.roll(value, 2 * wide - COL_TERMS * g, 1))
        pair = jnp.concatenate(split(jnp.concatenate(halves, axis=0)), axis=1)
        for unit in range(2):
            pltpu.matmul_acc_lhs(accs[unit], pair, load_staged_rhs=0)
        x = pltpu.matmul_pop(accs[0]) + pltpu.matmul_pop(accs[1])
        for k in range(n_sub):
            high_part, low_part = split(x[deep * k : deep * (k + 1)])
            pltpu.matmul_push_rhs(
                jnp.concatenate([high_part, low_part, high_part, low_part], axis=0), 0, k
            )
            pltpu.matmul_acc_lhs(accs[k], umat[...], load_staged_rhs=0)
        for k in range(n_sub):
            y = pltpu.matmul_pop(accs[k])
            out_ref[k, 0] = y[:ub, :vb] - y[ub:, vb:]
            out_ref[k, 1] = y[:ub, vb:] + y[ub:, :vb]

    pl.run_scoped(subgrids, *[pltpu.ACC(unit)((2 * ub, MXU), f32) for unit in range(2)])
    sent = outbox.at[0 : HALF * (n_row * n_col - 1), :]
    pltpu.make_async_copy(sent, sent, ssem).wait()


def fused_local(n_row, n_col, image, *rest):
    facet = image.shape[1]
    n_sub = rest[6].shape[0]
    wide, deep = n_col * COL_TERMS, n_row * ROW_TERMS
    ub, vb = SG // n_row, SG // n_col
    f32, b16, i32 = jnp.float32, jnp.bfloat16, jnp.int32
    vmem, smem, dma = pltpu.VMEM, pltpu.SMEM, pltpu.SemaphoreType.DMA
    rest = [rest[0].reshape(1, -1), rest[1].reshape(1, -1), *rest[2:]]
    held = pl.pallas_call(
        functools.partial(fused_kernel, (n_row, n_col, n_sub, facet, SG)),
        out_shape=vmem((n_sub, 2, ub, vb), f32),
        in_specs=[pl.BlockSpec(memory_space=pl.ANY)] * 9,
        out_specs=pl.BlockSpec(memory_space=vmem),
        scratch_shapes=[
            vmem((facet, 2 * facet), b16),
            vmem((2 * n_sub * wide, 2 * facet), b16),
            vmem((n_sub, 2 * deep, facet), b16),
            vmem((32, facet), f32),
            vmem((2, n_sub * n_row, facet), f32),
            vmem((2, n_sub * n_col, facet), f32),
            vmem((facet, 2 * n_sub * wide), b16),
            vmem((n_col * HALF * n_row, 2 * wide), f32),
            vmem((n_col * HALF * n_row, 2 * wide), f32),
            vmem((8 * wide, 2 * vb), b16),
            vmem((2 * ub, 4 * deep), b16),
            *[vmem(a.shape, a.dtype) for a in rest[:2]],
            *[smem(a.shape, a.dtype) for a in rest[2:]],
            dma((2,)),
            dma((8,)),
            dma,
            dma,
        ],
        compiler_params=pltpu.CompilerParams(
            collective_id=0, has_side_effects=True, vmem_limit_bytes=56 << 20
        ),
    )(image, *rest)
    return held


def solution(mesh):
    n_row, n_col = mesh.shape["frow"], mesh.shape["fcol"]
    ub, vb = SG // n_row, SG // n_col

    def local(image, *rest):
        facet, n_sub = image.shape[1], rest[-1].shape[0]
        tiled = (
            SG == ub * n_row == vb * n_col
            and n_row % 4 == 0
            and n_col == 2 * n_sub
            and n_col * COL_TERMS == 64
            and ub % 8 == 0
            and vb % 128 == 0
            and image.shape[2] == facet
            and facet == 2 * MXU
            and 2 * n_row * ROW_TERMS == facet // 4
            and 2 * n_sub * n_col * COL_TERMS == MXU
            and n_sub == 2
            and 4 * ub == 2 * vb == 4 * n_row * ROW_TERMS == MXU
            and remainder(facet // 2, ub // 2, ROW_TERMS) < 2.0**-24
            and remainder(facet // 2, vb // 2, COL_TERMS) < 2.0**-24
        )
        return (functools.partial(fused_local, n_row, n_col) if tiled else general_local)(image, *rest)

    placed = (P(None, "frow", "fcol"), P("frow"), P("fcol"), P(), P(), P(), P(), P(), P())
    return jax.shard_map(
        local, mesh=mesh, in_specs=placed, out_specs=P(None, None, "frow", "fcol"), check_vma=False
    )
```

```python
import functools
import math

import jax
import jax.numpy as jnp
from jax import lax
from jax.experimental import pallas as pl
from jax.experimental.pallas import tpu as pltpu
from jax.sharding import PartitionSpec as P

SG = 512
IMAGE = 65536


def phase_index(first, second):
    high = first * (second // 256) % 256 * 256
    return (high + first * (second % 256)) % 65536


def dft_table(coords, freqs):
    angle = phase_index(coords, freqs).astype(jnp.float32) * (2.0 * math.pi / IMAGE)
    return (jnp.cos(angle).astype(jnp.bfloat16), (-jnp.sin(angle)).astype(jnp.bfloat16))


def coord_unit(coords):
    return (coords % IMAGE).astype(jnp.float32) / IMAGE - 0.5


def block_table(table_re, table_im):
    upper = jnp.concatenate([table_re, table_im], axis=1)
    lower = jnp.concatenate([-table_im, table_re], axis=1)
    return jnp.concatenate([upper, lower], axis=0)


def general_local(
    image,
    window_rows,
    window_cols,
    w_terms,
    facet_row_offset,
    facet_col_offset,
    band_offset,
    sub_row_offset,
    sub_column,
):
    facet = image.shape[1]
    column_count = band_offset.shape[0]
    sub_count = sub_row_offset.shape[0]
    frow_index = lax.axis_index("frow")
    fcol_index = lax.axis_index("fcol")
    freq_base = jnp.arange(SG, dtype=jnp.int32)
    gcol = facet_col_offset[fcol_index] + jnp.arange(image.shape[2], dtype=jnp.int32)
    mcoord = coord_unit(gcol)
    row_base = facet_row_offset[frow_index]
    row_ids = row_base + jnp.arange(facet, dtype=jnp.int32)
    radius = coord_unit(row_ids)[:, None] ** 2 + mcoord[None, :] ** 2
    scale = window_rows[:, None] * window_cols[None, :]
    first = image[0].astype(jnp.float32) * scale
    second = image[1].astype(jnp.float32) * scale
    prepared = []
    for column in range(column_count):
        angle = w_terms[column] * radius
        cosine = jnp.cos(angle)
        sine = jnp.sin(angle)
        prep_re = (first * cosine - second * sine).astype(jnp.bfloat16)
        prep_im = (first * sine + second * cosine).astype(jnp.bfloat16)
        prepared.append(jnp.concatenate([prep_re, prep_im], axis=1))
    band_dev = SG // lax.axis_size("fcol")
    freqs = jnp.arange(band_dev * lax.axis_size("fcol"), dtype=jnp.int32)
    outputs = []
    for column in range(column_count):
        table_re, table_im = dft_table(gcol[:, None], band_offset[column] + freqs[None, :])
        whole_table = block_table(table_re, table_im)
        product = lax.dot_general(
            whole_table,
            prepared[column],
            (((0,), (1,)), ((), ())),
            preferred_element_type=jnp.float32,
        )
        outputs.append(
            product.reshape(2, band_dev * lax.axis_size("fcol"), facet).transpose(1, 0, 2)
        )
    summed = lax.psum_scatter(jnp.stack(outputs, axis=1), "fcol", scatter_dimension=0, tiled=True)
    banded = (summed / math.sqrt(facet * lax.axis_size("fcol"))).astype(jnp.bfloat16)
    chosen = jnp.take(banded, sub_column, axis=1)
    right_side = chosen.transpose(1, 2, 3, 0).reshape(sub_count, 2 * facet, band_dev)
    table_re, table_im = dft_table(
        row_ids[None, :, None], sub_row_offset[:, None, None] + freq_base[None, None, :]
    )
    left_real = jnp.concatenate([table_re, -table_im], axis=1)
    left_imag = jnp.concatenate([table_im, table_re], axis=1)
    left_side = jnp.stack([left_real, left_imag], axis=2)
    term = jnp.einsum("kxcu,kxv->kcuv", left_side, right_side, preferred_element_type=jnp.float32)
    term = term * (1.0 / math.sqrt(facet * lax.axis_size("frow")))
    return lax.psum_scatter(term, "frow", scatter_dimension=2, tiled=True)


MESH = pl.DeviceIdType.MESH
TAU = 2.0 * math.pi
ROW_TERMS = 8
COL_TERMS = 16
HALF = ROW_TERMS // 2
BESSEL_STEPS = 8
MXU = 256


def remainder(half_facet, half_block, terms):
    z_max = TAU * half_facet * half_block / IMAGE
    return 2.0 * (z_max / 2.0) ** terms / math.factorial(terms)


def iota(shape, axis):
    return lax.broadcasted_iota(jnp.int32, shape, axis)


def turn(index):
    return (index & (IMAGE - 1)).astype(jnp.float32) * (1.0 / IMAGE)


def phasor(turns):
    quadrant = jnp.floor(turns * 4.0 + 0.5)
    t = (turns - quadrant * 0.25) * TAU
    s = t * t
    sine = t * (1.0 + s * (-1 / 6 + s * (1 / 120 + s * (-1 / 5040 + s * (1 / 362880)))))
    cosine = 1.0 + s * (-1 / 2 + s * (1 / 24 + s * (-1 / 720 + s * (1 / 40320 + s * (-1 / 3628800)))))
    q = quadrant.astype(jnp.int32)
    odd = (q & 1) == 1
    real = jnp.where(odd, sine, cosine)
    imag = jnp.where(odd, cosine, sine)
    real = jnp.where(((q + 1) & 2) == 2, -real, real)
    imag = jnp.where((q & 2) == 2, -imag, imag)
    return real, imag


def coord_square(coords):
    unit = (coords & (IMAGE - 1)).astype(jnp.float32) * (1.0 / IMAGE) - 0.5
    return unit * unit


def bessel(order, z, terms):
    half = z * 0.5
    q = half * half
    lead = jnp.where(order == 0, 1.0, 2.0)
    for i in range(1, terms):
        lead = jnp.where(order >= i, lead * half * (1.0 / i), lead)
    tail = jnp.ones_like(z)
    for j in range(BESSEL_STEPS, 0, -1):
        tail = 1.0 - tail * q / (j * (order + j)).astype(jnp.float32)
    return lead * tail


def split(value):
    high = value.astype(jnp.bfloat16)
    return high, (value - high.astype(jnp.float32)).astype(jnp.bfloat16)


def fused_kernel(
    dims,
    image_hbm, wrow_hbm, wcol_hbm, w_hbm, row_off_hbm, col_off_hbm, band_hbm, sub_off_hbm, sub_col_hbm,
    out_ref,
    pixels, right, rtab, cheb, rphase, cphase, outbox, inbox, vmat, umat,
    wrow_ref, wcol_ref, w_ref, row_off_ref, col_off_ref, band_ref, sub_off_ref, sub_col_ref,
    isem, lsem, ssem, rsem,
):
    n_row, n_col, n_sub, facet, sg = dims
    r = lax.axis_index("frow")
    c = lax.axis_index("fcol")
    ub, vb = sg // n_row, sg // n_col
    center = facet // 2
    wide = n_col * COL_TERMS
    full = n_sub * wide
    deep = n_row * ROW_TERMS
    tall = HALF * n_row
    f32, b16 = jnp.float32, jnp.bfloat16

    images = [
        [
            pltpu.make_async_copy(
                image_hbm.at[i, MXU * t : MXU * (t + 1), :],
                pixels.at[i, MXU * t : MXU * (t + 1), :],
                isem.at[i, t],
            )
            for t in range(facet // MXU)
        ]
        for i in range(2)
    ]
    smalls = [
        pltpu.make_async_copy(src, dst, lsem)
        for i, (src, dst) in enumerate(
            [
                (sub_col_hbm, sub_col_ref),
                (w_hbm, w_ref),
                (band_hbm, band_ref),
                (sub_off_hbm, sub_off_ref),
                (row_off_hbm, row_off_ref),
                (col_off_hbm, col_off_ref),
                (wrow_hbm, wrow_ref),
                (wcol_hbm, wcol_ref),
            ]
        )
    ]
    for copy in smalls:
        copy.start()
    for copy in images[0]:
        copy.start()

    order = [(dr, dc) for dr in list(range(2, n_row)) + [1, 0] for dc in list(range(1, n_col)) + [0]]
    order = [at for at in order if at != (0, 0)]
    barrier = pltpu.get_barrier_semaphore()
    for number, (dr, dc) in enumerate(order):
        if number == 12:
            for copy in images[1]:
                copy.start()
        peer = ((r + dr) % n_row, (c + dc) % n_col)
        pl.semaphore_signal(barrier, inc=1, device_id=peer, device_id_type=MESH)

    lane = iota((8, facet), 1)
    local = (lane - center).astype(f32) * (1.0 / center)
    sub = iota((8, facet), 0)
    before, now = jnp.ones_like(local), local
    low = jnp.where(sub == 0, before, now)
    high = low
    for n in range(2, COL_TERMS):
        before, now = now, 2.0 * local * now - before
        if n < 8:
            low = jnp.where(sub == n, now, low)
        else:
            high = jnp.where(sub == n - 8, now, high)
    cheb[0:8, :] = low
    cheb[8:16, :] = high
    for h in range(2):
        part = cheb[HALF * h : HALF * (h + 1), :]
        cheb[16 + 8 * h : 24 + 8 * h, :] = jnp.concatenate([part, part], axis=0)

    for copy in smalls:
        copy.wait()
    columns = [sub_col_ref[k] for k in range(n_sub)]

    def by_sub(index, values):
        out = jnp.full(index.shape, values[0])
        for k in range(1, n_sub):
            out = jnp.where(index == k, values[k], out)
        return out

    waves = [w_ref[columns[k]] * (1.0 / TAU) for k in range(n_sub)]

    def phases(table, coords, n_block, block, firsts, shift, gain):
        row = iota((n_sub * n_block, facet), 0)
        which = row // n_block
        start = by_sub(which, firsts) + ((row + shift) % n_block) * block + block // 2
        turns = by_sub(which, waves) * coord_square(coords) - turn(coords * start)
        re, im = phasor(turns)
        table[0] = re * gain
        table[1] = im * gain

    gcol = col_off_ref[c] + iota((1, facet), 1)
    grow = row_off_ref[r] + iota((1, facet), 1)
    scale = 1.0 / math.sqrt(facet * n_col) / math.sqrt(facet * n_row)
    def column_tables():
        phases(cphase, gcol, n_col, vb, [band_ref[columns[k]] for k in range(n_sub)], c, wcol_ref[...])
        basis = cheb[0:COL_TERMS, :]
        for k in range(n_sub):
            for p in range(n_col):
                at = k * n_col + p
                re = (cphase[0, at : at + 1, :] * basis).astype(b16)
                im = (cphase[1, at : at + 1, :] * basis).astype(b16)
                top = wide * k + COL_TERMS * p
                right[top : top + COL_TERMS, :facet] = re
                right[top : top + COL_TERMS, facet:] = -im
                right[top + full : top + full + COL_TERMS, :facet] = im
                right[top + full : top + full + COL_TERMS, facet:] = re

    phases(rphase, grow, n_row, ub, [sub_off_ref[k] for k in range(n_sub)], 0, wrow_ref[...] * scale)
    groups, group = n_row // 2, 2 * n_sub * 2 * ROW_TERMS
    terms = cheb[16:32, :]
    first_half = sub < HALF
    for b in range(groups):
        for k in range(n_sub):
            at = k * n_row + 2 * b
            re, im = (
                jnp.where(first_half, rphase[i, at : at + 1, :], rphase[i, at + 1 : at + 2, :])
                for i in range(2)
            )
            re = (jnp.concatenate([re, re], axis=0) * terms).astype(b16)
            im = (jnp.concatenate([im, im], axis=0) * terms).astype(b16)
            top = group * b + 2 * ROW_TERMS * k
            low = top + group // 2
            rtab[0, top : top + 2 * ROW_TERMS, :] = re
            rtab[0, low : low + 2 * ROW_TERMS, :] = im
            rtab[1, top : top + 2 * ROW_TERMS, :] = -im
            rtab[1, low : low + 2 * ROW_TERMS, :] = re

    slot = iota((tall, full), 1) // COL_TERMS

    def rows_of(d, i):
        return pl.ds(tall * d + HALF * i, HALF)

    def send(to):
        for at in range(n_col):

            @pl.when(jnp.logical_or(r != to, c != at))
            def _():
                d = (at + n_col - c) % n_col
                pltpu.make_async_remote_copy(
                    src_ref=outbox.at[rows_of(d, to), :],
                    dst_ref=inbox.at[rows_of(d, r), :],
                    send_sem=ssem,
                    recv_sem=rsem,
                    device_id=(to, at),
                    device_id_type=MESH,
                ).start()

    def moments(*accs):
        accs = [accs[groups * i : groups * (i + 1)] for i in range(4)]
        sums, totals = accs[:2], accs[2:]

        column_tables()
        for i in range(2):
            for t in range(facet // MXU):
                images[i][t].wait()
                for unit in range(2):
                    pltpu.matmul_push_rhs(
                        pixels[i, MXU * t : MXU * (t + 1), MXU * unit : MXU * (unit + 1)], t, unit
                    )
                for b in range(groups):
                    for unit in range(2):
                        pltpu.matmul_acc_lhs(
                            sums[unit][b],
                            rtab[i, group * b : group * (b + 1), MXU * t : MXU * (t + 1)],
                            load_staged_rhs=t if b == 0 else None,
                        )

        def push(i):
            for unit in range(2):
                at = i * facet + MXU * unit
                pltpu.matmul_push_rhs(right[:, at : at + MXU], i, unit, transpose=True)

        def contract(b, i, unit, value, load):
            part = value[group // 2 * i : group // 2 * (i + 1)]
            pltpu.matmul_acc_lhs(totals[unit][b], part, load_staged_rhs=load)

        def pack(b):
            product = pltpu.matmul_pop(totals[0][b]) + pltpu.matmul_pop(totals[1][b])
            turned = []
            for g in range(4):
                h, i = g // 2, g % 2
                value = None
                for k in range(n_sub):
                    top = 2 * ROW_TERMS * k + ROW_TERMS * h
                    part = product[top : top + ROW_TERMS, full * i : full * (i + 1)]
                    value = part if k == 0 else jnp.where(slot[:8] // n_col == k, part, value)
                turned.append(value if g == 0 else pltpu.roll(value, COL_TERMS * g, 1))
            for d in range(n_col):
                box = turned[0]
                for g in range(1, 4):
                    box = jnp.where(slot[:8] % n_col == (d + g) % n_col, turned[g], box)
                outbox[tall * d + 8 * b : tall * d + 8 * (b + 1), :] = box

        push(0)
        push(1)
        values = [pltpu.matmul_pop(sums[unit][0]).astype(b16) for unit in range(2)]
        for i in range(2):
            for unit in range(2):
                contract(0, i, unit, values[unit], i)
        pack(0)
        pl.semaphore_wait(barrier, n_row * n_col - 1)
        for to in range(2):
            send(to)
        push(0)
        values = [
            [pltpu.matmul_pop(sums[unit][b]).astype(b16) for unit in range(2)] for b in range(1, groups)
        ]
        for i in (1, 0):
            for b in range(1, groups):
                for unit in range(2):
                    contract(b, i, unit, values[b - 1][unit], 0 if i == 0 and b == 1 else None)
        for b in range(1, groups):
            pack(b)

    pl.run_scoped(
        moments,
        *[
            pltpu.ACC(unit)((rows, MXU), f32)
            for rows in (group, group // 2)
            for unit in range(2)
            for _ in range(groups)
        ],
    )

    pltpu.make_async_copy(outbox.at[rows_of(0, r), :], inbox.at[rows_of(0, r), :], rsem).start()
    for to in range(2, n_row):
        send(to)

    row = iota((wide, vb), 0)
    off = iota((wide, vb), 1) - vb // 2
    which, term = row // COL_TERMS, row % COL_TERMS
    start = jnp.full((wide, vb), center)
    for p in range(n_col):
        start = jnp.where(which == p, col_off_ref[(c + n_col - p) % n_col] + center, start)
    re, im = phasor(-turn(start * off) - 0.25 * (term % 4).astype(f32))
    size = bessel(term, off.astype(f32) * (TAU * center / IMAGE), COL_TERMS)
    re, im = re * size, im * size
    blank = jnp.zeros((wide, 2 * vb), b16)
    for i, pair in enumerate(((re, im), (-im, re))):
        for j, part in enumerate(split(jnp.concatenate(pair, axis=1))):
            for k in range(n_sub):
                for other in range(n_sub):
                    top = full * i + wide * other
                    vmat[k, j, top : top + wide, :] = part if other == k else blank

    lanes = iota((ub, deep), 1)
    off = iota((ub, deep), 0) - ub // 2
    which = lanes // HALF % n_row
    term = lanes // (HALF * n_row) * HALF + lanes % HALF
    start = jnp.full((ub, deep), center)
    for b in range(n_row):
        start = jnp.where(which == b, row_off_ref[b] + center, start)
    re, im = phasor(-turn(start * off) - 0.25 * (term % 4).astype(f32))
    size = bessel(term, off.astype(f32) * (TAU * center / IMAGE), ROW_TERMS)
    for i, part in enumerate((re * size, im * size)):
        high_part, low_part = split(part)
        rows = slice(i * ub, (i + 1) * ub)
        for j, piece in enumerate((high_part, high_part, low_part, low_part)):
            umat[rows, deep * j : deep * (j + 1)] = piece

    def subgrids(*accs):
        for k in range(n_sub):
            for j in range(2):
                pltpu.matmul_push_rhs(vmat[k, j], j, k)
        pltpu.make_async_copy(inbox, inbox, rsem).wait()
        boxes = [inbox[tall * d : tall * (d + 1), :] for d in range(n_col)]
        parts = []
        for g in range(4):
            value = boxes[0]
            for d in range(1, n_col):
                value = jnp.where(slot % n_col == (d + g) % n_col, boxes[d], value)
            parts.append(value if g == 0 else pltpu.roll(value, full - COL_TERMS * g, 1))
        high_part, low_part = split(
            jnp.concatenate(
                [jnp.concatenate(parts[i::2], axis=0) for i in range(2)], axis=1
            )
        )
        for k in range(n_sub):
            pltpu.matmul_acc_lhs(accs[k], high_part, load_staged_rhs=0)
        for k in range(n_sub):
            pltpu.matmul_acc_lhs(accs[k], low_part)
        for k in range(n_sub):
            pltpu.matmul_acc_lhs(accs[k], high_part, load_staged_rhs=1)
        for k in range(n_sub):
            piece, rest = split(pltpu.matmul_pop(accs[k]))
            pltpu.matmul_push_rhs(jnp.concatenate([piece, rest, piece, rest], axis=0), 0, k)
            pltpu.matmul_acc_lhs(accs[n_sub + k], umat[...], load_staged_rhs=0)
        for k in range(n_sub):
            y = pltpu.matmul_pop(accs[n_sub + k])
            out_ref[k, 0] = y[:ub, :vb] - y[ub:, vb:]
            out_ref[k, 1] = y[:ub, vb:] + y[ub:, :vb]

    pl.run_scoped(
        subgrids,
        *[pltpu.ACC(unit)((rows, MXU), f32) for rows in (deep, 2 * ub) for unit in range(n_sub)],
    )
    sent = outbox.at[0 : HALF * (n_row * n_col - 1), :]
    pltpu.make_async_copy(sent, sent, ssem).wait()


def fused_local(n_row, n_col, image, *rest):
    facet = image.shape[1]
    n_sub = rest[6].shape[0]
    wide, deep = n_col * COL_TERMS, n_row * ROW_TERMS
    ub, vb = SG // n_row, SG // n_col
    f32, b16, i32 = jnp.float32, jnp.bfloat16, jnp.int32
    vmem, smem, dma = pltpu.VMEM, pltpu.SMEM, pltpu.SemaphoreType.DMA
    rest = [rest[0].reshape(1, -1), rest[1].reshape(1, -1), *rest[2:]]
    held = pl.pallas_call(
        functools.partial(fused_kernel, (n_row, n_col, n_sub, facet, SG)),
        out_shape=vmem((n_sub, 2, ub, vb), f32),
        in_specs=[pl.BlockSpec(memory_space=pl.ANY)] * 9,
        out_specs=pl.BlockSpec(memory_space=vmem),
        scratch_shapes=[
            vmem((2, facet, facet), b16),
            vmem((2 * n_sub * wide, 2 * facet), b16),
            vmem((2, 2 * n_sub * deep, facet), b16),
            vmem((32, facet), f32),
            vmem((2, n_sub * n_row, facet), f32),
            vmem((2, n_sub * n_col, facet), f32),
            vmem((n_col * HALF * n_row, n_sub * wide), f32),
            vmem((n_col * HALF * n_row, n_sub * wide), f32),
            vmem((n_sub, 2, 2 * n_sub * wide, 2 * vb), b16),
            vmem((2 * ub, 4 * deep), b16),
            *[vmem(a.shape, a.dtype) for a in rest[:2]],
            *[smem(a.shape, a.dtype) for a in rest[2:]],
            dma((2, facet // MXU)),
            dma,
            dma,
            dma,
        ],
        compiler_params=pltpu.CompilerParams(
            collective_id=0, has_side_effects=True, vmem_limit_bytes=56 << 20
        ),
    )(image, *rest)
    return held


def solution(mesh):
    n_row, n_col = mesh.shape["frow"], mesh.shape["fcol"]
    ub, vb = SG // n_row, SG // n_col

    def local(image, *rest):
        facet, n_sub = image.shape[1], rest[-1].shape[0]
        tiled = (
            SG == ub * n_row == vb * n_col
            and n_row % 4 == 0
            and n_col == 4
            and n_col * COL_TERMS == 64
            and ub % 8 == 0
            and vb % 128 == 0
            and image.shape[2] == facet
            and facet == 2 * MXU
            and 2 * n_sub * n_col * COL_TERMS == MXU
            and n_sub == 2
            and 4 * ub == 2 * vb == 4 * n_row * ROW_TERMS == MXU
            and remainder(facet // 2, ub // 2, ROW_TERMS) < 2.0**-24
            and remainder(facet // 2, vb // 2, COL_TERMS) < 2.0**-24
        )
        return (functools.partial(fused_local, n_row, n_col) if tiled else general_local)(image, *rest)

    placed = (P(None, "frow", "fcol"), P("frow"), P("fcol"), P(), P(), P(), P(), P(), P())
    return jax.shard_map(
        local, mesh=mesh, in_specs=placed, out_specs=P(None, None, "frow", "fcol"), check_vma=False
    )
```

```python
import functools
import math

import jax
import jax.numpy as jnp
from jax import lax
from jax.experimental import pallas as pl
from jax.experimental.pallas import tpu as pltpu
from jax.sharding import PartitionSpec as P

SG = 512
IMAGE = 65536


def phase_index(first, second):
    high = first * (second // 256) % 256 * 256
    return (high + first * (second % 256)) % 65536


def dft_table(coords, freqs):
    angle = phase_index(coords, freqs).astype(jnp.float32) * (2.0 * math.pi / IMAGE)
    return (jnp.cos(angle).astype(jnp.bfloat16), (-jnp.sin(angle)).astype(jnp.bfloat16))


def coord_unit(coords):
    return (coords % IMAGE).astype(jnp.float32) / IMAGE - 0.5


def block_table(table_re, table_im):
    upper = jnp.concatenate([table_re, table_im], axis=1)
    lower = jnp.concatenate([-table_im, table_re], axis=1)
    return jnp.concatenate([upper, lower], axis=0)


def general_local(
    image,
    window_rows,
    window_cols,
    w_terms,
    facet_row_offset,
    facet_col_offset,
    band_offset,
    sub_row_offset,
    sub_column,
):
    facet = image.shape[1]
    column_count = band_offset.shape[0]
    sub_count = sub_row_offset.shape[0]
    frow_index = lax.axis_index("frow")
    fcol_index = lax.axis_index("fcol")
    freq_base = jnp.arange(SG, dtype=jnp.int32)
    gcol = facet_col_offset[fcol_index] + jnp.arange(image.shape[2], dtype=jnp.int32)
    mcoord = coord_unit(gcol)
    row_base = facet_row_offset[frow_index]
    row_ids = row_base + jnp.arange(facet, dtype=jnp.int32)
    radius = coord_unit(row_ids)[:, None] ** 2 + mcoord[None, :] ** 2
    scale = window_rows[:, None] * window_cols[None, :]
    first = image[0].astype(jnp.float32) * scale
    second = image[1].astype(jnp.float32) * scale
    prepared = []
    for column in range(column_count):
        angle = w_terms[column] * radius
        cosine = jnp.cos(angle)
        sine = jnp.sin(angle)
        prep_re = (first * cosine - second * sine).astype(jnp.bfloat16)
        prep_im = (first * sine + second * cosine).astype(jnp.bfloat16)
        prepared.append(jnp.concatenate([prep_re, prep_im], axis=1))
    band_dev = SG // lax.axis_size("fcol")
    freqs = jnp.arange(band_dev * lax.axis_size("fcol"), dtype=jnp.int32)
    outputs = []
    for column in range(column_count):
        table_re, table_im = dft_table(gcol[:, None], band_offset[column] + freqs[None, :])
        whole_table = block_table(table_re, table_im)
        product = lax.dot_general(
            whole_table,
            prepared[column],
            (((0,), (1,)), ((), ())),
            preferred_element_type=jnp.float32,
        )
        outputs.append(
            product.reshape(2, band_dev * lax.axis_size("fcol"), facet).transpose(1, 0, 2)
        )
    summed = lax.psum_scatter(jnp.stack(outputs, axis=1), "fcol", scatter_dimension=0, tiled=True)
    banded = (summed / math.sqrt(facet * lax.axis_size("fcol"))).astype(jnp.bfloat16)
    chosen = jnp.take(banded, sub_column, axis=1)
    right_side = chosen.transpose(1, 2, 3, 0).reshape(sub_count, 2 * facet, band_dev)
    table_re, table_im = dft_table(
        row_ids[None, :, None], sub_row_offset[:, None, None] + freq_base[None, None, :]
    )
    left_real = jnp.concatenate([table_re, -table_im], axis=1)
    left_imag = jnp.concatenate([table_im, table_re], axis=1)
    left_side = jnp.stack([left_real, left_imag], axis=2)
    term = jnp.einsum("kxcu,kxv->kcuv", left_side, right_side, preferred_element_type=jnp.float32)
    term = term * (1.0 / math.sqrt(facet * lax.axis_size("frow")))
    return lax.psum_scatter(term, "frow", scatter_dimension=2, tiled=True)


MESH = pl.DeviceIdType.MESH
TAU = 2.0 * math.pi
ROW_TERMS = 8
COL_TERMS = 16
HALF = ROW_TERMS // 2
BESSEL_STEPS = 8
MXU = 256


def remainder(half_facet, half_block, terms):
    z_max = TAU * half_facet * half_block / IMAGE
    return 2.0 * (z_max / 2.0) ** terms / math.factorial(terms)


def iota(shape, axis):
    return lax.broadcasted_iota(jnp.int32, shape, axis)


def turn(index):
    return (index & (IMAGE - 1)).astype(jnp.float32) * (1.0 / IMAGE)


def phasor(turns):
    quadrant = jnp.floor(turns * 4.0 + 0.5)
    t = (turns - quadrant * 0.25) * TAU
    s = t * t
    sine = t * (1.0 + s * (-1 / 6 + s * (1 / 120 + s * (-1 / 5040 + s * (1 / 362880)))))
    cosine = 1.0 + s * (-1 / 2 + s * (1 / 24 + s * (-1 / 720 + s * (1 / 40320 + s * (-1 / 3628800)))))
    q = quadrant.astype(jnp.int32)
    odd = (q & 1) == 1
    real = jnp.where(odd, sine, cosine)
    imag = jnp.where(odd, cosine, sine)
    real = jnp.where(((q + 1) & 2) == 2, -real, real)
    imag = jnp.where((q & 2) == 2, -imag, imag)
    return real, imag


def coord_square(coords):
    unit = (coords & (IMAGE - 1)).astype(jnp.float32) * (1.0 / IMAGE) - 0.5
    return unit * unit


def bessel(order, z, terms):
    half = z * 0.5
    q = half * half
    lead = jnp.where(order == 0, 1.0, 2.0)
    for i in range(1, terms):
        lead = jnp.where(order >= i, lead * half * (1.0 / i), lead)
    tail = jnp.ones_like(z)
    for j in range(BESSEL_STEPS, 0, -1):
        tail = 1.0 - tail * q / (j * (order + j)).astype(jnp.float32)
    return lead * tail


def split(value):
    high = value.astype(jnp.bfloat16)
    return high, (value - high.astype(jnp.float32)).astype(jnp.bfloat16)


def fused_kernel(
    dims,
    image_hbm, wrow_hbm, wcol_hbm, w_hbm, row_off_hbm, col_off_hbm, band_hbm, sub_off_hbm, sub_col_hbm,
    out_ref,
    pixels, right, rtab, cheb, rphase, cphase, outbox, inbox, vmat, umat,
    wrow_ref, wcol_ref, w_ref, row_off_ref, col_off_ref, band_ref, sub_off_ref, sub_col_ref,
    isem, lsem, ssem, rsem,
):
    n_row, n_col, n_sub, facet, sg = dims
    r = lax.axis_index("frow")
    c = lax.axis_index("fcol")
    ub, vb = sg // n_row, sg // n_col
    center = facet // 2
    wide = n_col * COL_TERMS
    full = n_sub * wide
    deep = n_row * ROW_TERMS
    tall = HALF * n_row
    f32, b16 = jnp.float32, jnp.bfloat16

    images = [
        pltpu.make_async_copy(image_hbm.at[i], pixels.at[i], isem.at[i]) for i in range(2)
    ]
    smalls = [
        pltpu.make_async_copy(src, dst, lsem)
        for i, (src, dst) in enumerate(
            [
                (sub_col_hbm, sub_col_ref),
                (w_hbm, w_ref),
                (band_hbm, band_ref),
                (sub_off_hbm, sub_off_ref),
                (row_off_hbm, row_off_ref),
                (col_off_hbm, col_off_ref),
                (wrow_hbm, wrow_ref),
                (wcol_hbm, wcol_ref),
            ]
        )
    ]
    for copy in smalls:
        copy.start()
    images[0].start()

    order = [(dr, dc) for dr in list(range(2, n_row)) + [1, 0] for dc in list(range(1, n_col)) + [0]]
    order = [at for at in order if at != (0, 0)]
    barrier = pltpu.get_barrier_semaphore()
    for number, (dr, dc) in enumerate(order):
        if number == 4:
            images[1].start()
        peer = ((r + dr) % n_row, (c + dc) % n_col)
        pl.semaphore_signal(barrier, inc=1, device_id=peer, device_id_type=MESH)

    lane = iota((8, facet), 1)
    local = (lane - center).astype(f32) * (1.0 / center)
    sub = iota((8, facet), 0)
    before, now = jnp.ones_like(local), local
    low = jnp.where(sub == 0, before, now)
    high = low
    for n in range(2, COL_TERMS):
        before, now = now, 2.0 * local * now - before
        if n < 8:
            low = jnp.where(sub == n, now, low)
        else:
            high = jnp.where(sub == n - 8, now, high)
    cheb[0:8, :] = low
    cheb[8:16, :] = high
    for h in range(2):
        part = cheb[HALF * h : HALF * (h + 1), :]
        cheb[16 + 8 * h : 24 + 8 * h, :] = jnp.concatenate([part, part], axis=0)

    for copy in smalls:
        copy.wait()
    columns = [sub_col_ref[k] for k in range(n_sub)]

    def by_sub(index, values):
        out = jnp.full(index.shape, values[0])
        for k in range(1, n_sub):
            out = jnp.where(index == k, values[k], out)
        return out

    waves = [w_ref[columns[k]] * (1.0 / TAU) for k in range(n_sub)]

    def phases(table, coords, n_block, block, firsts, shift, gain):
        row = iota((n_sub * n_block, facet), 0)
        which = row // n_block
        start = by_sub(which, firsts) + ((row + shift) % n_block) * block + block // 2
        turns = by_sub(which, waves) * coord_square(coords) - turn(coords * start)
        re, im = phasor(turns)
        table[0] = re * gain
        table[1] = im * gain

    gcol = col_off_ref[c] + iota((1, facet), 1)
    grow = row_off_ref[r] + iota((1, facet), 1)
    scale = 1.0 / math.sqrt(facet * n_col) / math.sqrt(facet * n_row)
    def column_tables():
        phases(cphase, gcol, n_col, vb, [band_ref[columns[k]] for k in range(n_sub)], c, wcol_ref[...])
        basis = cheb[0:COL_TERMS, :]
        for k in range(n_sub):
            for p in range(n_col):
                at = k * n_col + p
                re = (cphase[0, at : at + 1, :] * basis).astype(b16)
                im = (cphase[1, at : at + 1, :] * basis).astype(b16)
                top = wide * k + COL_TERMS * p
                right[top : top + COL_TERMS, :facet] = re
                right[top : top + COL_TERMS, facet:] = -im
                right[top + full : top + full + COL_TERMS, :facet] = im
                right[top + full : top + full + COL_TERMS, facet:] = re

    phases(rphase, grow, n_row, ub, [sub_off_ref[k] for k in range(n_sub)], 0, wrow_ref[...] * scale)
    groups, group = n_row // 2, 2 * n_sub * 2 * ROW_TERMS
    terms = cheb[16:32, :]
    first_half = sub < HALF
    for b in range(groups):
        for k in range(n_sub):
            at = k * n_row + 2 * b
            re, im = (
                jnp.where(first_half, rphase[i, at : at + 1, :], rphase[i, at + 1 : at + 2, :])
                for i in range(2)
            )
            re = (jnp.concatenate([re, re], axis=0) * terms).astype(b16)
            im = (jnp.concatenate([im, im], axis=0) * terms).astype(b16)
            top = group * b + 2 * ROW_TERMS * k
            low = top + group // 2
            rtab[0, top : top + 2 * ROW_TERMS, :] = re
            rtab[0, low : low + 2 * ROW_TERMS, :] = im
            rtab[1, top : top + 2 * ROW_TERMS, :] = -im
            rtab[1, low : low + 2 * ROW_TERMS, :] = re

    slot = iota((tall, full), 1) // COL_TERMS

    def rows_of(d, i):
        return pl.ds(tall * d + HALF * i, HALF)

    def send(to):
        for at in range(n_col):

            @pl.when(jnp.logical_or(r != to, c != at))
            def _():
                d = (at + n_col - c) % n_col
                pltpu.make_async_remote_copy(
                    src_ref=outbox.at[rows_of(d, to), :],
                    dst_ref=inbox.at[rows_of(d, r), :],
                    send_sem=ssem,
                    recv_sem=rsem,
                    device_id=(to, at),
                    device_id_type=MESH,
                ).start()

    def moments(*accs):
        accs = [accs[groups * i : groups * (i + 1)] for i in range(4)]
        sums, totals = accs[:2], accs[2:]

        column_tables()
        for i in range(2):
            images[i].wait()
            for t in range(facet // MXU):
                for unit in range(2):
                    pltpu.matmul_push_rhs(
                        pixels[i, MXU * t : MXU * (t + 1), MXU * unit : MXU * (unit + 1)], t, unit
                    )
                for b in range(groups):
                    for unit in range(2):
                        pltpu.matmul_acc_lhs(
                            sums[unit][b],
                            rtab[i, group * b : group * (b + 1), MXU * t : MXU * (t + 1)],
                            load_staged_rhs=t if b == 0 else None,
                        )

        def push(i):
            for unit in range(2):
                at = i * facet + MXU * unit
                pltpu.matmul_push_rhs(right[:, at : at + MXU], i, unit, transpose=True)

        def contract(b, i, unit, value, load):
            part = value[group // 2 * i : group // 2 * (i + 1)]
            pltpu.matmul_acc_lhs(totals[unit][b], part, load_staged_rhs=load)

        def pack(b):
            product = pltpu.matmul_pop(totals[0][b]) + pltpu.matmul_pop(totals[1][b])
            turned = []
            for g in range(4):
                h, i = g // 2, g % 2
                value = None
                for k in range(n_sub):
                    top = 2 * ROW_TERMS * k + ROW_TERMS * h
                    part = product[top : top + ROW_TERMS, full * i : full * (i + 1)]
                    value = part if k == 0 else jnp.where(slot[:8] // n_col == k, part, value)
                turned.append(value if g == 0 else pltpu.roll(value, COL_TERMS * g, 1))
            for d in range(n_col):
                box = turned[0]
                for g in range(1, 4):
                    box = jnp.where(slot[:8] % n_col == (d + g) % n_col, turned[g], box)
                outbox[tall * d + 8 * b : tall * d + 8 * (b + 1), :] = box

        push(0)
        push(1)
        values = [pltpu.matmul_pop(sums[unit][0]).astype(b16) for unit in range(2)]
        for i in range(2):
            for unit in range(2):
                contract(0, i, unit, values[unit], i)
        pack(0)
        pl.semaphore_wait(barrier, n_row * n_col - 1)
        for to in range(2):
            send(to)
        push(0)
        values = [
            [pltpu.matmul_pop(sums[unit][b]).astype(b16) for unit in range(2)] for b in range(1, groups)
        ]
        for i in (1, 0):
            for b in range(1, groups):
                for unit in range(2):
                    contract(b, i, unit, values[b - 1][unit], 0 if i == 0 and b == 1 else None)
        for b in range(1, groups):
            pack(b)

    pl.run_scoped(
        moments,
        *[
            pltpu.ACC(unit)((rows, MXU), f32)
            for rows in (group, group // 2)
            for unit in range(2)
            for _ in range(groups)
        ],
    )

    pltpu.make_async_copy(outbox.at[rows_of(0, r), :], inbox.at[rows_of(0, r), :], rsem).start()
    for to in range(2, n_row):
        send(to)

    row = iota((wide, vb), 0)
    off = iota((wide, vb), 1) - vb // 2
    which, term = row // COL_TERMS, row % COL_TERMS
    start = jnp.full((wide, vb), center)
    for p in range(n_col):
        start = jnp.where(which == p, col_off_ref[(c + n_col - p) % n_col] + center, start)
    re, im = phasor(-turn(start * off) - 0.25 * (term % 4).astype(f32))
    size = bessel(term, off.astype(f32) * (TAU * center / IMAGE), COL_TERMS)
    re, im = re * size, im * size
    blank = jnp.zeros((wide, 2 * vb), b16)
    for i, pair in enumerate(((re, im), (-im, re))):
        for j, part in enumerate(split(jnp.concatenate(pair, axis=1))):
            for k in range(n_sub):
                for other in range(n_sub):
                    top = full * i + wide * other
                    vmat[k, j, top : top + wide, :] = part if other == k else blank

    lanes = iota((ub, deep), 1)
    off = iota((ub, deep), 0) - ub // 2
    which = lanes // HALF % n_row
    term = lanes // (HALF * n_row) * HALF + lanes % HALF
    start = jnp.full((ub, deep), center)
    for b in range(n_row):
        start = jnp.where(which == b, row_off_ref[b] + center, start)
    re, im = phasor(-turn(start * off) - 0.25 * (term % 4).astype(f32))
    size = bessel(term, off.astype(f32) * (TAU * center / IMAGE), ROW_TERMS)
    for i, part in enumerate((re * size, im * size)):
        high_part, low_part = split(part)
        rows = slice(i * ub, (i + 1) * ub)
        for j, piece in enumerate((high_part, high_part, low_part, low_part)):
            umat[rows, deep * j : deep * (j + 1)] = piece

    def subgrids(*accs):
        for k in range(n_sub):
            for j in range(2):
                pltpu.matmul_push_rhs(vmat[k, j], j, k)
        pltpu.make_async_copy(inbox, inbox, rsem).wait()
        boxes = [inbox[tall * d : tall * (d + 1), :] for d in range(n_col)]
        parts = []
        for g in range(4):
            value = boxes[0]
            for d in range(1, n_col):
                value = jnp.where(slot % n_col == (d + g) % n_col, boxes[d], value)
            parts.append(value if g == 0 else pltpu.roll(value, full - COL_TERMS * g, 1))
        high_part, low_part = split(
            jnp.concatenate(
                [jnp.concatenate(parts[i::2], axis=0) for i in range(2)], axis=1
            )
        )
        for k in range(n_sub):
            pltpu.matmul_acc_lhs(accs[k], high_part, load_staged_rhs=0)
        for k in range(n_sub):
            pltpu.matmul_acc_lhs(accs[k], low_part)
        for k in range(n_sub):
            pltpu.matmul_acc_lhs(accs[k], high_part, load_staged_rhs=1)
        for k in range(n_sub):
            piece, rest = split(pltpu.matmul_pop(accs[k]))
            pltpu.matmul_push_rhs(jnp.concatenate([piece, rest, piece, rest], axis=0), 0, k)
            pltpu.matmul_acc_lhs(accs[n_sub + k], umat[...], load_staged_rhs=0)
        for k in range(n_sub):
            y = pltpu.matmul_pop(accs[n_sub + k])
            out_ref[k, 0] = y[:ub, :vb] - y[ub:, vb:]
            out_ref[k, 1] = y[:ub, vb:] + y[ub:, :vb]

    pl.run_scoped(
        subgrids,
        *[pltpu.ACC(unit)((rows, MXU), f32) for rows in (deep, 2 * ub) for unit in range(n_sub)],
    )
    sent = outbox.at[0 : HALF * (n_row * n_col - 1), :]
    pltpu.make_async_copy(sent, sent, ssem).wait()


def fused_local(n_row, n_col, image, *rest):
    facet = image.shape[1]
    n_sub = rest[6].shape[0]
    wide, deep = n_col * COL_TERMS, n_row * ROW_TERMS
    ub, vb = SG // n_row, SG // n_col
    f32, b16, i32 = jnp.float32, jnp.bfloat16, jnp.int32
    vmem, smem, dma = pltpu.VMEM, pltpu.SMEM, pltpu.SemaphoreType.DMA
    rest = [rest[0].reshape(1, -1), rest[1].reshape(1, -1), *rest[2:]]
    held = pl.pallas_call(
        functools.partial(fused_kernel, (n_row, n_col, n_sub, facet, SG)),
        out_shape=vmem((n_sub, 2, ub, vb), f32),
        in_specs=[pl.BlockSpec(memory_space=pl.ANY)] * 9,
        out_specs=pl.BlockSpec(memory_space=vmem),
        scratch_shapes=[
            vmem((2, facet, facet), b16),
            vmem((2 * n_sub * wide, 2 * facet), b16),
            vmem((2, 2 * n_sub * deep, facet), b16),
            vmem((32, facet), f32),
            vmem((2, n_sub * n_row, facet), f32),
            vmem((2, n_sub * n_col, facet), f32),
            vmem((n_col * HALF * n_row, n_sub * wide), f32),
            vmem((n_col * HALF * n_row, n_sub * wide), f32),
            vmem((n_sub, 2, 2 * n_sub * wide, 2 * vb), b16),
            vmem((2 * ub, 4 * deep), b16),
            *[vmem(a.shape, a.dtype) for a in rest[:2]],
            *[smem(a.shape, a.dtype) for a in rest[2:]],
            dma((2,)),
            dma,
            dma,
            dma,
        ],
        compiler_params=pltpu.CompilerParams(
            collective_id=0, has_side_effects=True, vmem_limit_bytes=56 << 20
        ),
    )(image, *rest)
    return held


def solution(mesh):
    n_row, n_col = mesh.shape["frow"], mesh.shape["fcol"]
    ub, vb = SG // n_row, SG // n_col

    def local(image, *rest):
        facet, n_sub = image.shape[1], rest[-1].shape[0]
        tiled = (
            SG == ub * n_row == vb * n_col
            and n_row % 4 == 0
            and n_col == 4
            and n_col * COL_TERMS == 64
            and ub % 8 == 0
            and vb % 128 == 0
            and image.shape[2] == facet
            and facet == 2 * MXU
            and 2 * n_sub * n_col * COL_TERMS == MXU
            and n_sub == 2
            and 4 * ub == 2 * vb == 4 * n_row * ROW_TERMS == MXU
            and remainder(facet // 2, ub // 2, ROW_TERMS) < 2.0**-24
            and remainder(facet // 2, vb // 2, COL_TERMS) < 2.0**-24
        )
        return (functools.partial(fused_local, n_row, n_col) if tiled else general_local)(image, *rest)

    placed = (P(None, "frow", "fcol"), P("frow"), P("fcol"), P(), P(), P(), P(), P(), P())
    return jax.shard_map(
        local, mesh=mesh, in_specs=placed, out_specs=P(None, None, "frow", "fcol"), check_vma=False
    )
```

```python
import functools
import math

import jax
import jax.numpy as jnp
from jax import lax
from jax.experimental import pallas as pl
from jax.experimental.pallas import tpu as pltpu
from jax.sharding import PartitionSpec as P

SG = 512
IMAGE = 65536


def phase_index(first, second):
    high = first * (second // 256) % 256 * 256
    return (high + first * (second % 256)) % 65536


def dft_table(coords, freqs):
    angle = phase_index(coords, freqs).astype(jnp.float32) * (2.0 * math.pi / IMAGE)
    return (jnp.cos(angle).astype(jnp.bfloat16), (-jnp.sin(angle)).astype(jnp.bfloat16))


def coord_unit(coords):
    return (coords % IMAGE).astype(jnp.float32) / IMAGE - 0.5


def block_table(table_re, table_im):
    upper = jnp.concatenate([table_re, table_im], axis=1)
    lower = jnp.concatenate([-table_im, table_re], axis=1)
    return jnp.concatenate([upper, lower], axis=0)


def general_local(
    image,
    window_rows,
    window_cols,
    w_terms,
    facet_row_offset,
    facet_col_offset,
    band_offset,
    sub_row_offset,
    sub_column,
):
    facet = image.shape[1]
    column_count = band_offset.shape[0]
    sub_count = sub_row_offset.shape[0]
    frow_index = lax.axis_index("frow")
    fcol_index = lax.axis_index("fcol")
    freq_base = jnp.arange(SG, dtype=jnp.int32)
    gcol = facet_col_offset[fcol_index] + jnp.arange(image.shape[2], dtype=jnp.int32)
    mcoord = coord_unit(gcol)
    row_base = facet_row_offset[frow_index]
    row_ids = row_base + jnp.arange(facet, dtype=jnp.int32)
    radius = coord_unit(row_ids)[:, None] ** 2 + mcoord[None, :] ** 2
    scale = window_rows[:, None] * window_cols[None, :]
    first = image[0].astype(jnp.float32) * scale
    second = image[1].astype(jnp.float32) * scale
    prepared = []
    for column in range(column_count):
        angle = w_terms[column] * radius
        cosine = jnp.cos(angle)
        sine = jnp.sin(angle)
        prep_re = (first * cosine - second * sine).astype(jnp.bfloat16)
        prep_im = (first * sine + second * cosine).astype(jnp.bfloat16)
        prepared.append(jnp.concatenate([prep_re, prep_im], axis=1))
    band_dev = SG // lax.axis_size("fcol")
    freqs = jnp.arange(band_dev * lax.axis_size("fcol"), dtype=jnp.int32)
    outputs = []
    for column in range(column_count):
        table_re, table_im = dft_table(gcol[:, None], band_offset[column] + freqs[None, :])
        whole_table = block_table(table_re, table_im)
        product = lax.dot_general(
            whole_table,
            prepared[column],
            (((0,), (1,)), ((), ())),
            preferred_element_type=jnp.float32,
        )
        outputs.append(
            product.reshape(2, band_dev * lax.axis_size("fcol"), facet).transpose(1, 0, 2)
        )
    summed = lax.psum_scatter(jnp.stack(outputs, axis=1), "fcol", scatter_dimension=0, tiled=True)
    banded = (summed / math.sqrt(facet * lax.axis_size("fcol"))).astype(jnp.bfloat16)
    chosen = jnp.take(banded, sub_column, axis=1)
    right_side = chosen.transpose(1, 2, 3, 0).reshape(sub_count, 2 * facet, band_dev)
    table_re, table_im = dft_table(
        row_ids[None, :, None], sub_row_offset[:, None, None] + freq_base[None, None, :]
    )
    left_real = jnp.concatenate([table_re, -table_im], axis=1)
    left_imag = jnp.concatenate([table_im, table_re], axis=1)
    left_side = jnp.stack([left_real, left_imag], axis=2)
    term = jnp.einsum("kxcu,kxv->kcuv", left_side, right_side, preferred_element_type=jnp.float32)
    term = term * (1.0 / math.sqrt(facet * lax.axis_size("frow")))
    return lax.psum_scatter(term, "frow", scatter_dimension=2, tiled=True)


MESH = pl.DeviceIdType.MESH
TAU = 2.0 * math.pi
ROW_TERMS = 8
COL_TERMS = 16
HALF = ROW_TERMS // 2
BESSEL_STEPS = 8
MXU = 256


def remainder(half_facet, half_block, terms):
    z_max = TAU * half_facet * half_block / IMAGE
    return 2.0 * (z_max / 2.0) ** terms / math.factorial(terms)


def iota(shape, axis):
    return lax.broadcasted_iota(jnp.int32, shape, axis)


def turn(index):
    return (index & (IMAGE - 1)).astype(jnp.float32) * (1.0 / IMAGE)


def phasor(turns):
    quadrant = jnp.floor(turns * 4.0 + 0.5)
    t = (turns - quadrant * 0.25) * TAU
    s = t * t
    sine = t * (1.0 + s * (-1 / 6 + s * (1 / 120 + s * (-1 / 5040 + s * (1 / 362880)))))
    cosine = 1.0 + s * (-1 / 2 + s * (1 / 24 + s * (-1 / 720 + s * (1 / 40320 + s * (-1 / 3628800)))))
    q = quadrant.astype(jnp.int32)
    odd = (q & 1) == 1
    real = jnp.where(odd, sine, cosine)
    imag = jnp.where(odd, cosine, sine)
    real = jnp.where(((q + 1) & 2) == 2, -real, real)
    imag = jnp.where((q & 2) == 2, -imag, imag)
    return real, imag


def coord_square(coords):
    unit = (coords & (IMAGE - 1)).astype(jnp.float32) * (1.0 / IMAGE) - 0.5
    return unit * unit


def bessel(order, z, terms):
    half = z * 0.5
    q = half * half
    lead = jnp.where(order == 0, 1.0, 2.0)
    for i in range(1, terms):
        lead = jnp.where(order >= i, lead * half * (1.0 / i), lead)
    tail = jnp.ones_like(z)
    for j in range(BESSEL_STEPS, 0, -1):
        tail = 1.0 - tail * q / (j * (order + j)).astype(jnp.float32)
    return lead * tail


def split(value):
    high = value.astype(jnp.bfloat16)
    return high, (value - high.astype(jnp.float32)).astype(jnp.bfloat16)


def fused_kernel(
    dims,
    image_hbm, wrow_hbm, wcol_hbm, w_hbm, row_off_hbm, col_off_hbm, band_hbm, sub_off_hbm, sub_col_hbm,
    out_ref,
    pixels, right, rtab, cheb, rphase, cphase, outbox, inbox, vmat, umat,
    wrow_ref, wcol_ref, w_ref, row_off_ref, col_off_ref, band_ref, sub_off_ref, sub_col_ref,
    isem, lsem, ssem, rsem,
):
    n_row, n_col, n_sub, facet, sg = dims
    r = lax.axis_index("frow")
    c = lax.axis_index("fcol")
    ub, vb = sg // n_row, sg // n_col
    center = facet // 2
    wide = n_col * COL_TERMS
    full = n_sub * wide
    deep = n_row * ROW_TERMS
    tall = HALF * n_row
    f32, b16 = jnp.float32, jnp.bfloat16

    images = [
        pltpu.make_async_copy(image_hbm.at[i], pixels.at[i], isem.at[i]) for i in range(2)
    ]
    smalls = [
        pltpu.make_async_copy(src, dst, lsem)
        for i, (src, dst) in enumerate(
            [
                (sub_col_hbm, sub_col_ref),
                (w_hbm, w_ref),
                (band_hbm, band_ref),
                (sub_off_hbm, sub_off_ref),
                (row_off_hbm, row_off_ref),
                (col_off_hbm, col_off_ref),
                (wrow_hbm, wrow_ref),
                (wcol_hbm, wcol_ref),
            ]
        )
    ]
    for copy in smalls:
        copy.start()
    images[0].start()

    order = [(dr, dc) for dr in list(range(2, n_row)) + [1, 0] for dc in list(range(1, n_col)) + [0]]
    order = [at for at in order if at != (0, 0)]
    barrier = pltpu.get_barrier_semaphore()
    for number, (dr, dc) in enumerate(order):
        if number == 4:
            images[1].start()
        peer = ((r + dr) % n_row, (c + dc) % n_col)
        pl.semaphore_signal(barrier, inc=1, device_id=peer, device_id_type=MESH)

    lane = iota((8, facet), 1)
    local = (lane - center).astype(f32) * (1.0 / center)
    sub = iota((8, facet), 0)
    before, now = jnp.ones_like(local), local
    low = jnp.where(sub == 0, before, now)
    high = low
    for n in range(2, COL_TERMS):
        before, now = now, 2.0 * local * now - before
        if n < 8:
            low = jnp.where(sub == n, now, low)
        else:
            high = jnp.where(sub == n - 8, now, high)
    cheb[0:8, :] = low
    cheb[8:16, :] = high
    for h in range(2):
        part = cheb[HALF * h : HALF * (h + 1), :]
        cheb[16 + 8 * h : 24 + 8 * h, :] = jnp.concatenate([part, part], axis=0)

    for copy in smalls:
        copy.wait()
    columns = [sub_col_ref[k] for k in range(n_sub)]

    def by_sub(index, values):
        out = jnp.full(index.shape, values[0])
        for k in range(1, n_sub):
            out = jnp.where(index == k, values[k], out)
        return out

    waves = [w_ref[columns[k]] * (1.0 / TAU) for k in range(n_sub)]

    def phases(table, coords, n_block, block, firsts, shift, gain):
        row = iota((n_sub * n_block, facet), 0)
        which = row // n_block
        start = by_sub(which, firsts) + ((row + shift) % n_block) * block + block // 2
        turns = by_sub(which, waves) * coord_square(coords) - turn(coords * start)
        re, im = phasor(turns)
        table[0] = re * gain
        table[1] = im * gain

    gcol = col_off_ref[c] + iota((1, facet), 1)
    grow = row_off_ref[r] + iota((1, facet), 1)
    scale = 1.0 / math.sqrt(facet * n_col) / math.sqrt(facet * n_row)
    def column_tables():
        phases(cphase, gcol, n_col, vb, [band_ref[columns[k]] for k in range(n_sub)], c, wcol_ref[...])
        basis = cheb[0:COL_TERMS, :]
        for k in range(n_sub):
            for p in range(n_col):
                at = k * n_col + p
                re = (cphase[0, at : at + 1, :] * basis).astype(b16)
                im = (cphase[1, at : at + 1, :] * basis).astype(b16)
                top = wide * k + COL_TERMS * p
                right[top : top + COL_TERMS, :facet] = re
                right[top : top + COL_TERMS, facet:] = -im
                right[top + full : top + full + COL_TERMS, :facet] = im
                right[top + full : top + full + COL_TERMS, facet:] = re

    phases(rphase, grow, n_row, ub, [sub_off_ref[k] for k in range(n_sub)], 0, wrow_ref[...] * scale)
    groups, group = n_row // 2, 2 * n_sub * 2 * ROW_TERMS
    terms = cheb[16:32, :]
    first_half = sub < HALF
    for b in range(groups):
        for k in range(n_sub):
            at = k * n_row + 2 * b
            re, im = (
                jnp.where(first_half, rphase[i, at : at + 1, :], rphase[i, at + 1 : at + 2, :])
                for i in range(2)
            )
            re = (jnp.concatenate([re, re], axis=0) * terms).astype(b16)
            im = (jnp.concatenate([im, im], axis=0) * terms).astype(b16)
            top = group * b + 2 * ROW_TERMS * k
            low = top + group // 2
            rtab[0, top : top + 2 * ROW_TERMS, :] = re
            rtab[0, low : low + 2 * ROW_TERMS, :] = im
            rtab[1, top : top + 2 * ROW_TERMS, :] = -im
            rtab[1, low : low + 2 * ROW_TERMS, :] = re

    slot = iota((tall, full), 1) // COL_TERMS

    def rows_of(d, i):
        return pl.ds(tall * d + HALF * i, HALF)

    def send(to):
        for at in range(n_col):

            @pl.when(jnp.logical_or(r != to, c != at))
            def _():
                d = (at + n_col - c) % n_col
                pltpu.make_async_remote_copy(
                    src_ref=outbox.at[rows_of(d, to), :],
                    dst_ref=inbox.at[rows_of(d, r), :],
                    send_sem=ssem,
                    recv_sem=rsem,
                    device_id=(to, at),
                    device_id_type=MESH,
                ).start()

    def moments(*accs):
        accs = [accs[groups * i : groups * (i + 1)] for i in range(4)]
        sums, totals = accs[:2], accs[2:]

        column_tables()
        for i in range(2):
            images[i].wait()
            for t in range(facet // MXU):
                for unit in range(2):
                    pltpu.matmul_push_rhs(
                        pixels[i, MXU * t : MXU * (t + 1), MXU * unit : MXU * (unit + 1)], t, unit
                    )
                for b in range(groups):
                    for unit in range(2):
                        pltpu.matmul_acc_lhs(
                            sums[unit][b],
                            rtab[i, group * b : group * (b + 1), MXU * t : MXU * (t + 1)],
                            load_staged_rhs=t if b == 0 else None,
                        )

        def push(i):
            for unit in range(2):
                at = i * facet + MXU * unit
                pltpu.matmul_push_rhs(right[:, at : at + MXU], i, unit, transpose=True)

        def contract(b, i, unit, value, load):
            part = value[group // 2 * i : group // 2 * (i + 1)]
            pltpu.matmul_acc_lhs(totals[unit][b], part, load_staged_rhs=load)

        def pack(b):
            product = pltpu.matmul_pop(totals[0][b]) + pltpu.matmul_pop(totals[1][b])
            turned = []
            for g in range(4):
                h, i = g // 2, g % 2
                value = None
                for k in range(n_sub):
                    top = 2 * ROW_TERMS * k + ROW_TERMS * h
                    part = product[top : top + ROW_TERMS, full * i : full * (i + 1)]
                    value = part if k == 0 else jnp.where(slot[:8] // n_col == k, part, value)
                turned.append(value if g == 0 else pltpu.roll(value, COL_TERMS * g, 1))
            for d in range(n_col):
                box = turned[0]
                for g in range(1, 4):
                    box = jnp.where(slot[:8] % n_col == (d + g) % n_col, turned[g], box)
                outbox[tall * d + 8 * b : tall * d + 8 * (b + 1), :] = box

        push(0)
        push(1)
        values = [pltpu.matmul_pop(sums[unit][0]).astype(b16) for unit in range(2)]
        for i in range(2):
            for unit in range(2):
                contract(0, i, unit, values[unit], i)
        pack(0)
        pl.semaphore_wait(barrier, n_row * n_col - 1)
        for to in range(2):
            send(to)
        push(0)
        values = [
            [pltpu.matmul_pop(sums[unit][b]).astype(b16) for unit in range(2)] for b in range(1, groups)
        ]
        for i in (1, 0):
            for b in range(1, groups):
                for unit in range(2):
                    contract(b, i, unit, values[b - 1][unit], 0 if i == 0 and b == 1 else None)
        for b in range(1, groups):
            pack(b)

    pl.run_scoped(
        moments,
        *[
            pltpu.ACC(unit)((rows, MXU), f32)
            for rows in (group, group // 2)
            for unit in range(2)
            for _ in range(groups)
        ],
    )

    pltpu.make_async_copy(outbox.at[rows_of(0, r), :], inbox.at[rows_of(0, r), :], rsem).start()
    for to in range(2, n_row):
        send(to)

    row = iota((wide, vb), 0)
    off = iota((wide, vb), 1) - vb // 2
    which, term = row // COL_TERMS, row % COL_TERMS
    start = jnp.full((wide, vb), center)
    for p in range(n_col):
        start = jnp.where(which == p, col_off_ref[(c + n_col - p) % n_col] + center, start)
    re, im = phasor(-turn(start * off) - 0.25 * (term % 4).astype(f32))
    size = bessel(term, off.astype(f32) * (TAU * center / IMAGE), COL_TERMS)
    re, im = re * size, im * size
    blank = jnp.zeros((wide, 2 * vb), b16)
    for i, pair in enumerate(((re, im), (-im, re))):
        for j, part in enumerate(split(jnp.concatenate(pair, axis=1))):
            for k in range(n_sub):
                for other in range(n_sub):
                    top = full * i + wide * other
                    vmat[k, j, top : top + wide, :] = part if other == k else blank

    lanes = iota((ub, deep), 1)
    off = iota((ub, deep), 0) - ub // 2
    which = lanes // HALF % n_row
    term = lanes // (HALF * n_row) * HALF + lanes % HALF
    start = jnp.full((ub, deep), center)
    for b in range(n_row):
        start = jnp.where(which == b, row_off_ref[b] + center, start)
    re, im = phasor(-turn(start * off) - 0.25 * (term % 4).astype(f32))
    size = bessel(term, off.astype(f32) * (TAU * center / IMAGE), ROW_TERMS)
    for i, part in enumerate((re * size, im * size)):
        high_part, low_part = split(part)
        rows = slice(i * ub, (i + 1) * ub)
        for j, piece in enumerate((high_part, high_part, low_part, low_part)):
            umat[rows, deep * j : deep * (j + 1)] = piece

    def subgrids(*accs):
        for k in range(n_sub):
            for j in range(2):
                pltpu.matmul_push_rhs(vmat[k, j], j, k)
        pltpu.make_async_copy(inbox, inbox, rsem).wait()
        boxes = [inbox[tall * d : tall * (d + 1), :] for d in range(n_col)]
        parts = []
        for g in range(4):
            value = boxes[0]
            for d in range(1, n_col):
                value = jnp.where(slot % n_col == (d + g) % n_col, boxes[d], value)
            parts.append(value if g == 0 else pltpu.roll(value, full - COL_TERMS * g, 1))
        high_part, low_part = split(
            jnp.concatenate(
                [jnp.concatenate(parts[i::2], axis=0) for i in range(2)], axis=1
            )
        )
        for k in range(n_sub):
            pltpu.matmul_acc_lhs(accs[k], high_part, load_staged_rhs=1)
        for k in range(n_sub):
            pltpu.matmul_acc_lhs(accs[k], high_part, load_staged_rhs=0)
        for k in range(n_sub):
            pltpu.matmul_acc_lhs(accs[k], low_part)
        for k in range(n_sub):
            piece, rest = split(pltpu.matmul_pop(accs[k]))
            pltpu.matmul_push_rhs(jnp.concatenate([piece, rest, piece, rest], axis=0), 0, k)
            pltpu.matmul_acc_lhs(accs[n_sub + k], umat[...], load_staged_rhs=0)
        for k in range(n_sub):
            y = pltpu.matmul_pop(accs[n_sub + k])
            out_ref[k, 0] = y[:ub, :vb] - y[ub:, vb:]
            out_ref[k, 1] = y[:ub, vb:] + y[ub:, :vb]

    pl.run_scoped(
        subgrids,
        *[pltpu.ACC(unit)((rows, MXU), f32) for rows in (deep, 2 * ub) for unit in range(n_sub)],
    )
    sent = outbox.at[0 : HALF * (n_row * n_col - 1), :]
    pltpu.make_async_copy(sent, sent, ssem).wait()


def fused_local(n_row, n_col, image, *rest):
    facet = image.shape[1]
    n_sub = rest[6].shape[0]
    wide, deep = n_col * COL_TERMS, n_row * ROW_TERMS
    ub, vb = SG // n_row, SG // n_col
    f32, b16, i32 = jnp.float32, jnp.bfloat16, jnp.int32
    vmem, smem, dma = pltpu.VMEM, pltpu.SMEM, pltpu.SemaphoreType.DMA
    rest = [rest[0].reshape(1, -1), rest[1].reshape(1, -1), *rest[2:]]
    held = pl.pallas_call(
        functools.partial(fused_kernel, (n_row, n_col, n_sub, facet, SG)),
        out_shape=vmem((n_sub, 2, ub, vb), f32),
        in_specs=[pl.BlockSpec(memory_space=pl.ANY)] * 9,
        out_specs=pl.BlockSpec(memory_space=vmem),
        scratch_shapes=[
            vmem((2, facet, facet), b16),
            vmem((2 * n_sub * wide, 2 * facet), b16),
            vmem((2, 2 * n_sub * deep, facet), b16),
            vmem((32, facet), f32),
            vmem((2, n_sub * n_row, facet), f32),
            vmem((2, n_sub * n_col, facet), f32),
            vmem((n_col * HALF * n_row, n_sub * wide), f32),
            vmem((n_col * HALF * n_row, n_sub * wide), f32),
            vmem((n_sub, 2, 2 * n_sub * wide, 2 * vb), b16),
            vmem((2 * ub, 4 * deep), b16),
            *[vmem(a.shape, a.dtype) for a in rest[:2]],
            *[smem(a.shape, a.dtype) for a in rest[2:]],
            dma((2,)),
            dma,
            dma,
            dma,
        ],
        compiler_params=pltpu.CompilerParams(
            collective_id=0, has_side_effects=True, vmem_limit_bytes=56 << 20
        ),
    )(image, *rest)
    return held


def solution(mesh):
    n_row, n_col = mesh.shape["frow"], mesh.shape["fcol"]
    ub, vb = SG // n_row, SG // n_col

    def local(image, *rest):
        facet, n_sub = image.shape[1], rest[-1].shape[0]
        tiled = (
            SG == ub * n_row == vb * n_col
            and n_row % 4 == 0
            and n_col == 4
            and n_col * COL_TERMS == 64
            and ub % 8 == 0
            and vb % 128 == 0
            and image.shape[2] == facet
            and facet == 2 * MXU
            and 2 * n_sub * n_col * COL_TERMS == MXU
            and n_sub == 2
            and 4 * ub == 2 * vb == 4 * n_row * ROW_TERMS == MXU
            and remainder(facet // 2, ub // 2, ROW_TERMS) < 2.0**-24
            and remainder(facet // 2, vb // 2, COL_TERMS) < 2.0**-24
        )
        return (functools.partial(fused_local, n_row, n_col) if tiled else general_local)(image, *rest)

    placed = (P(None, "frow", "fcol"), P("frow"), P("fcol"), P(), P(), P(), P(), P(), P())
    return jax.shard_map(
        local, mesh=mesh, in_specs=placed, out_specs=P(None, None, "frow", "fcol"), check_vma=False
    )
```

```python
import functools
import math

import jax
import jax.numpy as jnp
from jax import lax
from jax.experimental import pallas as pl
from jax.experimental.pallas import tpu as pltpu
from jax.sharding import PartitionSpec as P

SG = 512
IMAGE = 65536


def phase_index(first, second):
    high = first * (second // 256) % 256 * 256
    return (high + first * (second % 256)) % 65536


def dft_table(coords, freqs):
    angle = phase_index(coords, freqs).astype(jnp.float32) * (2.0 * math.pi / IMAGE)
    return (jnp.cos(angle).astype(jnp.bfloat16), (-jnp.sin(angle)).astype(jnp.bfloat16))


def coord_unit(coords):
    return (coords % IMAGE).astype(jnp.float32) / IMAGE - 0.5


def block_table(table_re, table_im):
    upper = jnp.concatenate([table_re, table_im], axis=1)
    lower = jnp.concatenate([-table_im, table_re], axis=1)
    return jnp.concatenate([upper, lower], axis=0)


def general_local(
    image,
    window_rows,
    window_cols,
    w_terms,
    facet_row_offset,
    facet_col_offset,
    band_offset,
    sub_row_offset,
    sub_column,
):
    facet = image.shape[1]
    column_count = band_offset.shape[0]
    sub_count = sub_row_offset.shape[0]
    frow_index = lax.axis_index("frow")
    fcol_index = lax.axis_index("fcol")
    freq_base = jnp.arange(SG, dtype=jnp.int32)
    gcol = facet_col_offset[fcol_index] + jnp.arange(image.shape[2], dtype=jnp.int32)
    mcoord = coord_unit(gcol)
    row_base = facet_row_offset[frow_index]
    row_ids = row_base + jnp.arange(facet, dtype=jnp.int32)
    radius = coord_unit(row_ids)[:, None] ** 2 + mcoord[None, :] ** 2
    scale = window_rows[:, None] * window_cols[None, :]
    first = image[0].astype(jnp.float32) * scale
    second = image[1].astype(jnp.float32) * scale
    prepared = []
    for column in range(column_count):
        angle = w_terms[column] * radius
        cosine = jnp.cos(angle)
        sine = jnp.sin(angle)
        prep_re = (first * cosine - second * sine).astype(jnp.bfloat16)
        prep_im = (first * sine + second * cosine).astype(jnp.bfloat16)
        prepared.append(jnp.concatenate([prep_re, prep_im], axis=1))
    band_dev = SG // lax.axis_size("fcol")
    freqs = jnp.arange(band_dev * lax.axis_size("fcol"), dtype=jnp.int32)
    outputs = []
    for column in range(column_count):
        table_re, table_im = dft_table(gcol[:, None], band_offset[column] + freqs[None, :])
        whole_table = block_table(table_re, table_im)
        product = lax.dot_general(
            whole_table,
            prepared[column],
            (((0,), (1,)), ((), ())),
            preferred_element_type=jnp.float32,
        )
        outputs.append(
            product.reshape(2, band_dev * lax.axis_size("fcol"), facet).transpose(1, 0, 2)
        )
    summed = lax.psum_scatter(jnp.stack(outputs, axis=1), "fcol", scatter_dimension=0, tiled=True)
    banded = (summed / math.sqrt(facet * lax.axis_size("fcol"))).astype(jnp.bfloat16)
    chosen = jnp.take(banded, sub_column, axis=1)
    right_side = chosen.transpose(1, 2, 3, 0).reshape(sub_count, 2 * facet, band_dev)
    table_re, table_im = dft_table(
        row_ids[None, :, None], sub_row_offset[:, None, None] + freq_base[None, None, :]
    )
    left_real = jnp.concatenate([table_re, -table_im], axis=1)
    left_imag = jnp.concatenate([table_im, table_re], axis=1)
    left_side = jnp.stack([left_real, left_imag], axis=2)
    term = jnp.einsum("kxcu,kxv->kcuv", left_side, right_side, preferred_element_type=jnp.float32)
    term = term * (1.0 / math.sqrt(facet * lax.axis_size("frow")))
    return lax.psum_scatter(term, "frow", scatter_dimension=2, tiled=True)


MESH = pl.DeviceIdType.MESH
TAU = 2.0 * math.pi
ROW_TERMS = 8
COL_TERMS = 16
HALF = ROW_TERMS // 2
BESSEL_STEPS = 8
MXU = 256


def remainder(half_facet, half_block, terms):
    z_max = TAU * half_facet * half_block / IMAGE
    return 2.0 * (z_max / 2.0) ** terms / math.factorial(terms)


def iota(shape, axis):
    return lax.broadcasted_iota(jnp.int32, shape, axis)


def turn(index):
    return (index & (IMAGE - 1)).astype(jnp.float32) * (1.0 / IMAGE)


def phasor(turns):
    quadrant = jnp.floor(turns * 4.0 + 0.5)
    t = (turns - quadrant * 0.25) * TAU
    s = t * t
    sine = t * (1.0 + s * (-1 / 6 + s * (1 / 120 + s * (-1 / 5040 + s * (1 / 362880)))))
    cosine = 1.0 + s * (-1 / 2 + s * (1 / 24 + s * (-1 / 720 + s * (1 / 40320 + s * (-1 / 3628800)))))
    q = quadrant.astype(jnp.int32)
    odd = (q & 1) == 1
    real = jnp.where(odd, sine, cosine)
    imag = jnp.where(odd, cosine, sine)
    real = jnp.where(((q + 1) & 2) == 2, -real, real)
    imag = jnp.where((q & 2) == 2, -imag, imag)
    return real, imag


def coord_square(coords):
    unit = (coords & (IMAGE - 1)).astype(jnp.float32) * (1.0 / IMAGE) - 0.5
    return unit * unit


def bessel(order, z, terms):
    half = z * 0.5
    q = half * half
    lead = jnp.where(order == 0, 1.0, 2.0)
    for i in range(1, terms):
        lead = jnp.where(order >= i, lead * half * (1.0 / i), lead)
    tail = jnp.ones_like(z)
    for j in range(BESSEL_STEPS, 0, -1):
        tail = 1.0 - tail * q / (j * (order + j)).astype(jnp.float32)
    return lead * tail


def split(value):
    high = value.astype(jnp.bfloat16)
    return high, (value - high.astype(jnp.float32)).astype(jnp.bfloat16)


def fused_kernel(
    dims,
    image_hbm, wrow_hbm, wcol_hbm, w_hbm, row_off_hbm, col_off_hbm, band_hbm, sub_off_hbm, sub_col_hbm,
    out_ref,
    pixels, right, rtab, cheb, rphase, cphase, outbox, inbox, vmat, umat,
    wrow_ref, wcol_ref, w_ref, row_off_ref, col_off_ref, band_ref, sub_off_ref, sub_col_ref,
    isem, lsem, ssem, rsem,
):
    n_row, n_col, n_sub, facet, sg = dims
    r = lax.axis_index("frow")
    c = lax.axis_index("fcol")
    ub, vb = sg // n_row, sg // n_col
    center = facet // 2
    wide = n_col * COL_TERMS
    full = n_sub * wide
    deep = n_row * ROW_TERMS
    tall = HALF * n_row
    f32, b16 = jnp.float32, jnp.bfloat16

    images = [
        pltpu.make_async_copy(image_hbm.at[i], pixels.at[i], isem.at[i]) for i in range(2)
    ]
    smalls = [
        pltpu.make_async_copy(src, dst, lsem)
        for i, (src, dst) in enumerate(
            [
                (sub_col_hbm, sub_col_ref),
                (w_hbm, w_ref),
                (band_hbm, band_ref),
                (sub_off_hbm, sub_off_ref),
                (row_off_hbm, row_off_ref),
                (col_off_hbm, col_off_ref),
                (wrow_hbm, wrow_ref),
                (wcol_hbm, wcol_ref),
            ]
        )
    ]
    for copy in smalls:
        copy.start()
    images[0].start()

    order = [(dr, dc) for dr in list(range(2, n_row)) + [1, 0] for dc in list(range(1, n_col)) + [0]]
    order = [at for at in order if at != (0, 0)]
    barrier = pltpu.get_barrier_semaphore()
    for number, (dr, dc) in enumerate(order):
        if number == 4:
            images[1].start()
        peer = ((r + dr) % n_row, (c + dc) % n_col)
        pl.semaphore_signal(barrier, inc=1, device_id=peer, device_id_type=MESH)

    lane = iota((8, facet), 1)
    local = (lane - center).astype(f32) * (1.0 / center)
    sub = iota((8, facet), 0)
    before, now = jnp.ones_like(local), local
    low = jnp.where(sub == 0, before, now)
    high = low
    for n in range(2, COL_TERMS):
        before, now = now, 2.0 * local * now - before
        if n < 8:
            low = jnp.where(sub == n, now, low)
        else:
            high = jnp.where(sub == n - 8, now, high)
    cheb[0:8, :] = low
    cheb[8:16, :] = high
    for h in range(2):
        part = cheb[HALF * h : HALF * (h + 1), :]
        cheb[16 + 8 * h : 24 + 8 * h, :] = jnp.concatenate([part, part], axis=0)

    for copy in smalls:
        copy.wait()
    columns = [sub_col_ref[k] for k in range(n_sub)]

    def by_sub(index, values):
        out = jnp.full(index.shape, values[0])
        for k in range(1, n_sub):
            out = jnp.where(index == k, values[k], out)
        return out

    waves = [w_ref[columns[k]] * (1.0 / TAU) for k in range(n_sub)]

    def phases(table, coords, n_block, block, firsts, shift, gain):
        row = iota((n_sub * n_block, facet), 0)
        which = row // n_block
        start = by_sub(which, firsts) + ((row + shift) % n_block) * block + block // 2
        turns = by_sub(which, waves) * coord_square(coords) - turn(coords * start)
        re, im = phasor(turns)
        table[0] = re * gain
        table[1] = im * gain

    gcol = col_off_ref[c] + iota((1, facet), 1)
    grow = row_off_ref[r] + iota((1, facet), 1)
    scale = 1.0 / math.sqrt(facet * n_col) / math.sqrt(facet * n_row)
    def column_tables():
        phases(cphase, gcol, n_col, vb, [band_ref[columns[k]] for k in range(n_sub)], c, wcol_ref[...])
        basis = cheb[0:COL_TERMS, :]
        for k in range(n_sub):
            for p in range(n_col):
                at = k * n_col + p
                re = (cphase[0, at : at + 1, :] * basis).astype(b16)
                im = (cphase[1, at : at + 1, :] * basis).astype(b16)
                top = wide * k + COL_TERMS * p
                right[top : top + COL_TERMS, :facet] = re
                right[top : top + COL_TERMS, facet:] = -im
                right[top + full : top + full + COL_TERMS, :facet] = im
                right[top + full : top + full + COL_TERMS, facet:] = re

    phases(rphase, grow, n_row, ub, [sub_off_ref[k] for k in range(n_sub)], 0, wrow_ref[...] * scale)
    groups, group = n_row // 2, 2 * n_sub * 2 * ROW_TERMS
    terms = cheb[16:32, :]
    first_half = sub < HALF
    for b in range(groups):
        for k in range(n_sub):
            at = k * n_row + 2 * b
            re, im = (
                jnp.where(first_half, rphase[i, at : at + 1, :], rphase[i, at + 1 : at + 2, :])
                for i in range(2)
            )
            re = (jnp.concatenate([re, re], axis=0) * terms).astype(b16)
            im = (jnp.concatenate([im, im], axis=0) * terms).astype(b16)
            top = group * b + 2 * ROW_TERMS * k
            low = top + group // 2
            rtab[0, top : top + 2 * ROW_TERMS, :] = re
            rtab[0, low : low + 2 * ROW_TERMS, :] = im
            rtab[1, top : top + 2 * ROW_TERMS, :] = -im
            rtab[1, low : low + 2 * ROW_TERMS, :] = re

    slot = iota((tall, full), 1) // COL_TERMS

    def rows_of(d, i):
        return pl.ds(tall * d + HALF * i, HALF)

    def send(to):
        for at in range(n_col):

            @pl.when(jnp.logical_or(r != to, c != at))
            def _():
                d = (at + n_col - c) % n_col
                pltpu.make_async_remote_copy(
                    src_ref=outbox.at[rows_of(d, to), :],
                    dst_ref=inbox.at[rows_of(d, r), :],
                    send_sem=ssem,
                    recv_sem=rsem,
                    device_id=(to, at),
                    device_id_type=MESH,
                ).start()

    def moments(*accs):
        accs = [accs[groups * i : groups * (i + 1)] for i in range(4)]
        sums, totals = accs[:2], accs[2:]

        column_tables()
        for i in range(2):
            images[i].wait()
            for t in range(facet // MXU):
                for unit in range(2):
                    pltpu.matmul_push_rhs(
                        pixels[i, MXU * t : MXU * (t + 1), MXU * unit : MXU * (unit + 1)], t, unit
                    )
                for b in range(groups):
                    for unit in range(2):
                        pltpu.matmul_acc_lhs(
                            sums[unit][b],
                            rtab[i, group * b : group * (b + 1), MXU * t : MXU * (t + 1)],
                            load_staged_rhs=t if b == 0 else None,
                        )

        def push(i):
            for unit in range(2):
                at = i * facet + MXU * unit
                pltpu.matmul_push_rhs(right[:, at : at + MXU], i, unit, transpose=True)

        def contract(b, i, unit, value, load):
            part = value[group // 2 * i : group // 2 * (i + 1)]
            pltpu.matmul_acc_lhs(totals[unit][b], part, load_staged_rhs=load)

        def pack(b):
            product = pltpu.matmul_pop(totals[0][b]) + pltpu.matmul_pop(totals[1][b])
            turned = []
            for g in range(4):
                h, i = g // 2, g % 2
                value = None
                for k in range(n_sub):
                    top = 2 * ROW_TERMS * k + ROW_TERMS * h
                    part = product[top : top + ROW_TERMS, full * i : full * (i + 1)]
                    value = part if k == 0 else jnp.where(slot[:8] // n_col == k, part, value)
                turned.append(value if g == 0 else pltpu.roll(value, COL_TERMS * g, 1))
            for d in range(n_col):
                box = turned[0]
                for g in range(1, 4):
                    box = jnp.where(slot[:8] % n_col == (d + g) % n_col, turned[g], box)
                outbox[tall * d + 8 * b : tall * d + 8 * (b + 1), :] = box

        push(0)
        push(1)
        values = [pltpu.matmul_pop(sums[unit][0]).astype(b16) for unit in range(2)]
        for i in range(2):
            for unit in range(2):
                contract(0, i, unit, values[unit], i)
        pack(0)
        pl.semaphore_wait(barrier, n_row * n_col - 1)
        for to in range(2):
            send(to)
        push(0)
        values = [
            [pltpu.matmul_pop(sums[unit][b]).astype(b16) for unit in range(2)] for b in range(1, groups)
        ]
        for i in (1, 0):
            for b in range(1, groups):
                for unit in range(2):
                    contract(b, i, unit, values[b - 1][unit], 0 if i == 0 and b == 1 else None)
        for b in range(1, groups):
            pack(b)

    pl.run_scoped(
        moments,
        *[
            pltpu.ACC(unit)((rows, MXU), f32)
            for rows in (group, group // 2)
            for unit in range(2)
            for _ in range(groups)
        ],
    )

    pltpu.make_async_copy(outbox.at[rows_of(0, r), :], inbox.at[rows_of(0, r), :], rsem).start()
    for to in range(2, n_row):
        send(to)

    row = iota((wide, vb), 0)
    off = iota((wide, vb), 1) - vb // 2
    which, term = row // COL_TERMS, row % COL_TERMS
    start = jnp.full((wide, vb), center)
    for p in range(n_col):
        start = jnp.where(which == p, col_off_ref[(c + n_col - p) % n_col] + center, start)
    re, im = phasor(-turn(start * off) - 0.25 * (term % 4).astype(f32))
    size = bessel(term, off.astype(f32) * (TAU * center / IMAGE), COL_TERMS)
    re, im = re * size, im * size
    blank = jnp.zeros((wide, 2 * vb), b16)
    for i, pair in enumerate(((re, im), (-im, re))):
        for j, part in enumerate(split(jnp.concatenate(pair, axis=1))):
            for k in range(n_sub):
                for other in range(n_sub):
                    top = full * i + wide * other
                    vmat[k, j, top : top + wide, :] = part if other == k else blank

    lanes = iota((ub, deep), 1)
    off = iota((ub, deep), 0) - ub // 2
    which = lanes // HALF % n_row
    term = lanes // (HALF * n_row) * HALF + lanes % HALF
    start = jnp.full((ub, deep), center)
    for b in range(n_row):
        start = jnp.where(which == b, row_off_ref[b] + center, start)
    re, im = phasor(-turn(start * off) - 0.25 * (term % 4).astype(f32))
    size = bessel(term, off.astype(f32) * (TAU * center / IMAGE), ROW_TERMS)
    for i, part in enumerate((re * size, im * size)):
        high_part, low_part = split(part)
        rows = slice(i * ub, (i + 1) * ub)
        for j, piece in enumerate((high_part, high_part, low_part, low_part)):
            umat[rows, deep * j : deep * (j + 1)] = piece

    def subgrids(*accs):
        for k in range(n_sub):
            for j in range(2):
                pltpu.matmul_push_rhs(vmat[k, j], j, k)
        pltpu.make_async_copy(inbox, inbox, rsem).wait()
        boxes = [inbox[tall * d : tall * (d + 1), :] for d in range(n_col)]
        parts = []
        for g in range(4):
            value = boxes[0]
            for d in range(1, n_col):
                value = jnp.where(slot % n_col == (d + g) % n_col, boxes[d], value)
            parts.append(value if g == 0 else pltpu.roll(value, full - COL_TERMS * g, 1))
        high_part, low_part = split(
            jnp.concatenate(
                [jnp.concatenate(parts[i::2], axis=0) for i in range(2)], axis=1
            )
        )
        for k in range(n_sub):
            pltpu.matmul_acc_lhs(accs[k], high_part, load_staged_rhs=1)
        for k in range(n_sub):
            pltpu.matmul_acc_lhs(accs[k], high_part, load_staged_rhs=0)
        for k in range(n_sub):
            pltpu.matmul_acc_lhs(accs[k], low_part)
        for k in range(n_sub):
            piece, rest = split(pltpu.matmul_pop(accs[k]))
            pltpu.matmul_push_rhs(jnp.concatenate([piece, rest, piece, rest], axis=0), 0, k)
            pltpu.matmul_acc_lhs(accs[n_sub + k], umat[...], load_staged_rhs=0)
        for k in range(n_sub):
            y = pltpu.matmul_pop(accs[n_sub + k])
            out_ref[k, 0] = y[:ub, :vb] - y[ub:, vb:]
            out_ref[k, 1] = y[:ub, vb:] + y[ub:, :vb]

    pl.run_scoped(
        subgrids,
        *[pltpu.ACC(unit)((rows, MXU), f32) for rows in (deep, 2 * ub) for unit in range(n_sub)],
    )
    sent = outbox.at[0 : HALF * (n_row * n_col - 1), :]
    pltpu.make_async_copy(sent, sent, ssem).wait()


def store_kernel(held, out_hbm, sem):
    copy = pltpu.make_async_copy(held, out_hbm, sem)
    copy.start()
    copy.wait()


def fused_local(n_row, n_col, image, *rest):
    facet = image.shape[1]
    n_sub = rest[6].shape[0]
    wide, deep = n_col * COL_TERMS, n_row * ROW_TERMS
    ub, vb = SG // n_row, SG // n_col
    f32, b16, i32 = jnp.float32, jnp.bfloat16, jnp.int32
    vmem, smem, dma = pltpu.VMEM, pltpu.SMEM, pltpu.SemaphoreType.DMA
    rest = [rest[0].reshape(1, -1), rest[1].reshape(1, -1), *rest[2:]]
    held = pl.pallas_call(
        functools.partial(fused_kernel, (n_row, n_col, n_sub, facet, SG)),
        out_shape=vmem((n_sub, 2, ub, vb), f32),
        in_specs=[pl.BlockSpec(memory_space=pl.ANY)] * 9,
        out_specs=pl.BlockSpec(memory_space=vmem),
        scratch_shapes=[
            vmem((2, facet, facet), b16),
            vmem((2 * n_sub * wide, 2 * facet), b16),
            vmem((2, 2 * n_sub * deep, facet), b16),
            vmem((32, facet), f32),
            vmem((2, n_sub * n_row, facet), f32),
            vmem((2, n_sub * n_col, facet), f32),
            vmem((n_col * HALF * n_row, n_sub * wide), f32),
            vmem((n_col * HALF * n_row, n_sub * wide), f32),
            vmem((n_sub, 2, 2 * n_sub * wide, 2 * vb), b16),
            vmem((2 * ub, 4 * deep), b16),
            *[vmem(a.shape, a.dtype) for a in rest[:2]],
            *[smem(a.shape, a.dtype) for a in rest[2:]],
            dma((2,)),
            dma,
            dma,
            dma,
        ],
        compiler_params=pltpu.CompilerParams(
            collective_id=0, has_side_effects=True, vmem_limit_bytes=56 << 20
        ),
    )(image, *rest)
    return pl.pallas_call(
        store_kernel,
        out_shape=jax.ShapeDtypeStruct(held.shape, f32),
        in_specs=[pl.BlockSpec(memory_space=vmem)],
        out_specs=pl.BlockSpec(memory_space=pl.ANY),
        scratch_shapes=[dma],
    )(pltpu.with_memory_space_constraint(held, vmem))


def solution(mesh):
    n_row, n_col = mesh.shape["frow"], mesh.shape["fcol"]
    ub, vb = SG // n_row, SG // n_col

    def local(image, *rest):
        facet, n_sub = image.shape[1], rest[-1].shape[0]
        tiled = (
            SG == ub * n_row == vb * n_col
            and n_row % 4 == 0
            and n_col == 4
            and n_col * COL_TERMS == 64
            and ub % 8 == 0
            and vb % 128 == 0
            and image.shape[2] == facet
            and facet == 2 * MXU
            and 2 * n_sub * n_col * COL_TERMS == MXU
            and n_sub == 2
            and 4 * ub == 2 * vb == 4 * n_row * ROW_TERMS == MXU
            and remainder(facet // 2, ub // 2, ROW_TERMS) < 2.0**-24
            and remainder(facet // 2, vb // 2, COL_TERMS) < 2.0**-24
        )
        return (functools.partial(fused_local, n_row, n_col) if tiled else general_local)(image, *rest)

    placed = (P(None, "frow", "fcol"), P("frow"), P("fcol"), P(), P(), P(), P(), P(), P())
    return jax.shard_map(
        local, mesh=mesh, in_specs=placed, out_specs=P(None, None, "frow", "fcol"), check_vma=False
    )
```
